32 devices in a mesh: ens: 2 (over x), band: 16 (over z, y, core).
Axes of the slice: x: 2, y: 2, z: 4, core: 2. Of those that a mesh axis runs over, the one named last changes fastest.
Arguments:
- atm_state: bfloat16 [256, 128, 384], P(('ens', 'band')), parts along dimension 0, may hold values from -6 to 6
- ocean_state: bfloat16 [256, 128, 384], P(('ens', 'band')), parts along dimension 0, may hold values from -6 to 6
- dw_kernel: float32 [2, 7, 7, 384], replicated, may hold values from -0.875 to 0.875
- norm_gain: float32 [2, 384], replicated, may hold values from 0.1 to 1.9
- w_up: bfloat16 [2, 384, 1536], replicated, may hold values from -0.3125 to 0.3125
- b_up: float32 [2, 1536], replicated, may hold values from -3 to 3
- w_down: bfloat16 [2, 384, 1536], replicated, may hold values from -0.15625 to 0.15625
- flux_out: bfloat16 [384, 256], replicated, may hold values from -0.3125 to 0.3125
- flux_in: bfloat16 [256, 384], replicated, may hold values from -0.375 to 0.375
- partner: int32 [32], P('ens'), parts along dimension 0, may hold values from 0 to 15, each once
- remap: int32 [256], P('ens'), parts along dimension 0, may hold values from 0 to 7
- land_mask: int32 [256, 128], P(('ens', 'band')), parts along dimension 0, may hold values 0 or 1
Outputs:
- atm_next: bfloat16 [256, 128, 384], P(('ens', 'band')), parts along dimension 0
- ocean_next: bfloat16 [256, 128, 384], P(('ens', 'band')), parts along dimension 0
The draws below stay inside these ranges and needn't reach their ends.
There are 2 independent parts, one for each index of `ens`. The reference program is written for one: setup_inputs(seed, part) draws one part's arguments, and reference() takes and returns one part's arrays. A program takes and returns all parts, laid end to end along the dimension named above; an argument that names none is the same for every part. Nothing has to cross between parts.
Inputs may be any that keep to these rules, and one draw needn't show every extreme that they name: Each of the 16 atmosphere bands is the partner of exactly one ocean band.
All inputs are finite; a program needn't handle non-finite values. No bound on the sum of `land_mask` on one device may be relied on, other than what follows from the above.
Results may differ from the reference program's by a relative error of at most 0.0075.
Values may be sent and summed in bfloat16 or wider, within the bound.
No kernel may reach another device: no remote copies, remote signals or barrier semaphores. Data moves between devices by JAX's collectives and lax.ppermute only.
A program may use at most 64 MiB of HBM per device.

```python
import jax
import jax.numpy as jnp
from jax import lax

CH = 384
HID = 1536
FLUX = 256
ROWS = 8
LON = 128
BANDS = 16
LAT = 128


def with_ends(values, stream_key, least, high):
    index_at = [jax.random.randint(jax.random.fold_in(stream_key, axis), (), 0, length) for axis, length in enumerate(values.shape)]
    main_axis = values.shape.index(max(values.shape))
    beside = index_at[:main_axis] + [(index_at[main_axis] + 1) % values.shape[main_axis]] + index_at[main_axis + 1:]
    return values.at[tuple(index_at)].set(least).at[tuple(beside)].set(high)


def level_of(own_key, extent, shards, low, top_value):
    level = 1.0
    for dim, blocks in shards:
        steps = jax.random.uniform(jax.random.fold_in(jax.random.fold_in(own_key, 6), dim), (blocks,), jnp.float32, low / len(shards), top_value / len(shards))
        level = level * jnp.repeat(jnp.exp(steps), extent[dim] // blocks).reshape((-1,) + (1,) * (len(extent) - 1 - dim))
    return level


def noise(key, dims, scale, most, cuts=(), kind=jnp.bfloat16):
    level = level_of(key, dims, cuts, -0.22, 0.18) if cuts else 1.0
    entries = jax.random.normal(key, dims, jnp.float32) * scale * level
    return jnp.minimum(jnp.maximum(entries, -most), most).astype(kind)


def setup_inputs(seed: int = 0, part: int = 0) -> dict:
    arg_keys = jax.random.split(jax.random.key(seed), 13)
    own_keys = jax.random.split(jax.random.fold_in(arg_keys[12], part), 13)
    return {
        "atm_state": noise(own_keys[0], (LAT, LON, CH), 1.0, 6.0, ((0, 16),)),
        "ocean_state": noise(own_keys[1], (LAT, LON, CH), 1.0, 6.0, ((0, 16),)),
        "dw_kernel": noise(arg_keys[2], (2, 7, 7, CH), 49 ** -0.5, 0.875, (), jnp.float32),
        "norm_gain": jnp.clip(1.0 + 0.18 * jax.random.normal(arg_keys[3], (2, CH), jnp.float32), 0.1, 1.9),
        "w_up": noise(arg_keys[4], (2, CH, HID), CH ** -0.5, 0.3125),
        "b_up": noise(arg_keys[5], (2, HID), 0.5, 3.0, (), jnp.float32),
        "w_down": noise(arg_keys[6], (2, CH, HID), HID ** -0.5, 0.15625),
        "flux_out": noise(arg_keys[7], (CH, FLUX), CH ** -0.5, 0.3125),
        "flux_in": noise(arg_keys[8], (FLUX, CH), FLUX ** -0.5, 0.375),
        "partner": jax.random.permutation(own_keys[9], BANDS).astype(jnp.int32),
        "remap": with_ends(jax.random.randint(own_keys[10], (LAT,), 0, ROWS), jax.random.fold_in(own_keys[10], 1), 0, ROWS - 1).astype(jnp.int32),
        "land_mask": with_ends((jax.random.randint(own_keys[11], (LAT, LON), 0, 4) < 3).astype(jnp.int32), jax.random.fold_in(own_keys[11], 1), 0, 1),
    }


def depthwise(field, kernel):
    values = field.astype(jnp.float32)
    padded = jnp.pad(values, ((3, 3), (0, 0), (0, 0)))
    padded = jnp.concatenate([padded[:, -3:], padded, padded[:, :3]], axis=1)
    height, width = (field.shape[0], field.shape[1])
    total = jnp.zeros(values.shape, jnp.float32)
    for a in range(7):
        for b in range(7):
            total = total + kernel[a, b] * padded[a:a + height, b:b + width]
    return total

def mixer(field, kernel, gain, up_mat, up_bias, down_mat):
    conv = depthwise(field, kernel)
    center = lax.optimization_barrier(jnp.mean(conv, axis=-1, keepdims=True))
    spread = lax.optimization_barrier(jnp.mean((conv - center) ** 2, axis=-1, keepdims=True))
    normed = ((conv - center) * lax.rsqrt(spread + 1e-06) * gain).astype(jnp.bfloat16)
    blocks = normed.reshape(16, -1, CH)

    def single(tokens):
        hidden = jax.nn.gelu(jnp.dot(tokens, up_mat, preferred_element_type=jnp.float32) + up_bias, approximate=True).astype(jnp.bfloat16)
        return lax.dot_general(hidden, down_mat, (((1,), (1,)), ((), ())), preferred_element_type=jnp.float32)
    update = lax.map(single, blocks).reshape(field.shape)
    return (field.astype(jnp.float32) + update).astype(jnp.bfloat16)

def reference(atm_state, ocean_state, dw_kernel, norm_gain, w_up, b_up, w_down, flux_out, flux_in, partner, remap, land_mask):
    atm_next = mixer(atm_state, dw_kernel[0], norm_gain[0], w_up[0], b_up[0], w_down[0])
    surface = jnp.dot(atm_next.reshape(-1, CH), flux_out, preferred_element_type=jnp.float32).astype(jnp.bfloat16).reshape(LAT, LON, FLUX)
    indices = (jnp.repeat(partner, ROWS) * ROWS + remap).astype(jnp.int32)
    moved = jnp.take(surface, indices, axis=0)
    forcing = jnp.dot(moved.reshape(-1, FLUX), flux_in, preferred_element_type=jnp.float32).reshape(LAT, LON, CH)
    ocean_in = (ocean_state.astype(jnp.float32) + land_mask.astype(jnp.float32)[:, :, None] * forcing).astype(jnp.bfloat16)
    ocean_next = mixer(ocean_in, dw_kernel[1], norm_gain[1], w_up[1], b_up[1], w_down[1])
    return (atm_next, ocean_next)
```

```python
import functools

import jax
import jax.numpy as jnp
from jax import lax
from jax.experimental import pallas as pl
from jax.experimental.pallas import tpu as pltpu
from jax.sharding import PartitionSpec as P

LANES = 128
SUB = 8
TAPS = 7
PAD = TAPS // 2
TILE = 256
F32 = jnp.float32
BF16 = jnp.bfloat16
VMEM = pl.BlockSpec(memory_space=pltpu.VMEM)
ANY = pl.BlockSpec(memory_space=pl.ANY)
LIMIT = 24 << 20


def far(x):
    return pltpu.with_memory_space_constraint(x, pltpu.HBM)


def near(x):
    return pltpu.with_memory_space_constraint(x, pltpu.VMEM)


class Plan:
    def __init__(self, rows, taps):
        self.z_ops, self.k_ops, self.leaves = [], [], []
        self.z_index, self.k_index = {}, {}
        zs = [self.z(("row", m)) for m in range(rows + taps - 1)]
        ks = [self.k(("tap", a)) for a in range(taps)]
        self.outs = self.fast(zs, ks, rows)

    def z(self, op):
        if op not in self.z_index:
            self.z_index[op] = len(self.z_ops)
            self.z_ops.append(op)
        return self.z_index[op]

    def k(self, op):
        if op not in self.k_index:
            self.k_index[op] = len(self.k_ops)
            self.k_ops.append(op)
        return self.k_index[op]

    def leaf(self, z, k):
        self.leaves.append((z, k))
        return ("leaf", len(self.leaves) - 1)

    def fast(self, zs, ks, count):
        if count % 2 or len(ks) == 1:
            outs = []
            for i in range(count):
                node = self.leaf(zs[i], ks[0])
                for j in range(1, len(ks)):
                    node = ("add", node, self.leaf(zs[i + j], ks[j]))
                outs.append(node)
            return outs
        half = count // 2
        even, odd, k0, k1 = zs[0::2], zs[1::2], ks[0::2], ks[1::2]
        both = [self.k(("add", k0[j], k1[j])) if j < len(k1) else k0[j] for j in range(len(k0))]
        need = half + len(k0) - 1
        first = self.fast(odd[:need], both, half)
        second = self.fast([self.z(("sub", even[n], odd[n])) for n in range(need)], k0, half)
        need = half + len(k1) - 1
        third = self.fast([self.z(("sub", even[n + 1], odd[n])) for n in range(need)], k1, half)
        outs = []
        for n in range(half):
            outs += [("add", first[n], second[n]), ("add", first[n], third[n])]
        return outs

    def rows_of(self, z):
        op = self.z_ops[z]
        return {op[1]} if op[0] == "row" else self.rows_of(op[1]) | self.rows_of(op[2])

    def split(self, known):
        early = [q for q, (z, _) in enumerate(self.leaves) if self.rows_of(z) <= set(known)]
        return early, [q for q in range(len(self.leaves)) if q not in early]


def tap_rows(kernel_ref, which, plan, leaves, weights):
    values = []
    for op in plan.k_ops:
        if op[0] == "tap":
            values.append(kernel_ref[op[1], :, which, :])
        else:
            values.append(values[op[1]] + values[op[2]])
    for n, q in enumerate(leaves):
        weights[n, 0:TAPS, :] = values[plan.leaves[q][1]]


def fill(load, plan, leaves, derived, width, lane_blocks):
    last = width // SUB - 1
    for block in range(width // SUB):
        for cb in range(lane_blocks):
            values = {}

            def node(z):
                if z not in values:
                    op = plan.z_ops[z]
                    if op[0] == "row":
                        values[z] = load(op[1], block, cb).astype(F32)
                    else:
                        values[z] = node(op[1]) - node(op[2])
                return values[z]

            for n, q in enumerate(leaves):
                value = node(plan.leaves[q][0])
                derived[cb, n, (block + 1) * SUB : (block + 2) * SUB, :] = value
                if block == 0:
                    derived[cb, n, width + SUB : width + 2 * SUB, :] = value
                if block == last:
                    derived[cb, n, 0:SUB, :] = value


def fir(derived, weights, cb, n, start, wide):
    lanes = slice(cb * LANES, (cb + 1) * LANES)
    total = [None] * wide
    for b in range(TAPS):
        weight = jnp.broadcast_to(weights[n, b : b + 1, lanes], (SUB, LANES))
        for v in range(wide):
            term = weight * derived[cb, n, pl.ds(start + (SUB - PAD + b + v * SUB), SUB), :]
            total[v] = term if total[v] is None else total[v] + term
    return total


def early_kernel(which, *refs):
    x_ref, kernel_hbm, early_ref, kernel, derived, weights, sem = refs
    rows, width, channels = x_ref.shape
    lane_blocks = channels // LANES
    plan = Plan(rows, TAPS)
    leaves, _ = plan.split(range(PAD, PAD + rows))
    copy = pltpu.make_async_copy(kernel_hbm, kernel, sem)
    copy.start()

    def load(m, block, cb):
        return x_ref[m - PAD, block * SUB : (block + 1) * SUB, cb * LANES : (cb + 1) * LANES]

    fill(load, plan, leaves, derived, width, lane_blocks)
    copy.wait()
    tap_rows(kernel, which, plan, leaves, weights)
    wide = 2 if width % (2 * SUB) == 0 else 1
    for cb in range(lane_blocks):

        @pl.loop(0, width // (wide * SUB))
        def _(step):
            start = pl.multiple_of(step * (wide * SUB), wide * SUB)
            for n in range(len(leaves)):
                for v, part in enumerate(fir(derived, weights, cb, n, start, wide)):
                    early_ref[cb, n, pl.ds(start + v * SUB, SUB), :] = part


def early(which, x, kernel):
    rows, width, channels = x.shape
    plan = Plan(rows, TAPS)
    leaves, _ = plan.split(range(PAD, PAD + rows))
    blocks = channels // LANES
    return pl.pallas_call(
        functools.partial(early_kernel, which),
        out_shape=pltpu.VMEM((blocks, len(leaves), width, LANES), F32),
        in_specs=[VMEM, ANY],
        out_specs=VMEM,
        scratch_shapes=[
            pltpu.VMEM(kernel.shape, F32),
            pltpu.VMEM((blocks, len(leaves), width + 2 * SUB, LANES), F32),
            pltpu.VMEM((len(leaves), SUB, channels), F32),
            pltpu.SemaphoreType.DMA,
        ],
        compiler_params=pltpu.CompilerParams(vmem_limit_bytes=12 << 20),
        cost_estimate=pl.CostEstimate(
            flops=40 * rows * width * channels, bytes_accessed=8 * rows * width * channels, transcendentals=0
        ),
        name=f"early{which}",
    )(near(x), far(kernel))


def gelu(u):
    half = 0.5 * u
    return half + half * jnp.tanh(u * (0.7978845608028654 + 0.035677408136300125 * (u * u)))


def mix_kernel(cfg, *refs):
    which, has_flux, split, prefetch = cfg
    refs = list(refs)
    x_ref, early_ref, one_ref, two_ref, odd_ref = [refs.pop(0) for _ in range(5)]
    kernel_hbm, gain_hbm, wu_hbm, bu_hbm, wd_hbm = [refs.pop(0) for _ in range(5)]
    fo_hbm = refs.pop(0) if has_flux else None
    sources = [refs.pop(0) for _ in range(prefetch)]
    out_hbm = refs.pop(0)
    surf_hbm = refs.pop(0) if has_flux else None
    targets = [refs.pop(0) for _ in range(prefetch)]
    kernel, gain, wu, bu, wd, derived, weights, conv, hidden, out, sem = refs[:11]
    rows, width, channels = x_ref.shape
    lane_blocks = channels // LANES
    plan = Plan(rows, TAPS)
    known, leaves = plan.split(range(PAD, PAD + rows))

    load_kernel = pltpu.make_async_copy(kernel_hbm, kernel, sem.at[0])
    late = [
        pltpu.make_async_copy(gain_hbm, gain, sem.at[1]),
        pltpu.make_async_copy(bu_hbm, bu, sem.at[2]),
        pltpu.make_async_copy(wu_hbm.at[which], wu, sem.at[3]),
        pltpu.make_async_copy(wd_hbm.at[which], wd, sem.at[4]),
    ]
    if has_flux:
        fo, surf = refs[11:]
        late.append(pltpu.make_async_copy(fo_hbm, fo, sem.at[5]))
    ahead = [
        pltpu.make_async_copy(source, target, sem.at[6 + n])
        for n, (source, target) in enumerate(zip(sources, targets))
    ]
    load_kernel.start()
    for copy in late + ahead:
        copy.start()

    odd = odd_ref[0] == 1

    def load(m, block, cb):
        lons, lanes = slice(block * SUB, (block + 1) * SUB), slice(cb * LANES, (cb + 1) * LANES)
        if PAD <= m < PAD + rows:
            return x_ref[m - PAD, lons, lanes]
        r = m if m < PAD else m - PAD - rows
        one, two = one_ref[r, lons, lanes].astype(F32), two_ref[r, lons, lanes].astype(F32)
        return jnp.where(odd, one, two) if m < PAD else jnp.where(odd, two, one)

    fill(load, plan, leaves, derived, width, lane_blocks)
    load_kernel.wait()
    tap_rows(kernel, which, plan, leaves, weights)
    wide = 2 if width % (2 * SUB) == 0 else 1
    for cb in range(lane_blocks):
        lanes = slice(cb * LANES, (cb + 1) * LANES)

        @pl.loop(0, width // (wide * SUB))
        def _(step):
            start = pl.multiple_of(step * (wide * SUB), wide * SUB)
            done = {}

            def value(node):
                if node not in done:
                    if node[0] == "add":
                        left, right = value(node[1]), value(node[2])
                        done[node] = [a + b for a, b in zip(left, right)]
                    elif node[1] in known:
                        n = known.index(node[1])
                        done[node] = [
                            early_ref[cb, n, pl.ds(start + v * SUB, SUB), :] for v in range(wide)
                        ]
                    else:
                        done[node] = fir(derived, weights, cb, leaves.index(node[1]), start, wide)
                return done[node]

            for i, node in enumerate(plan.outs):
                for v, part in enumerate(value(node)):
                    conv[i, pl.ds(start + v * SUB, SUB), lanes] = part

    for copy in late:
        copy.wait()
    group = rows // 2 if rows % 2 == 0 else rows
    cells = group * width
    stores = []
    for g in range(rows // group):
        part = slice(g * group, (g + 1) * group)
        total = conv[part].reshape(cells, channels)
        center = jnp.mean(total, axis=-1, keepdims=True)
        total = total - center
        spread = jnp.mean(total * total, axis=-1, keepdims=True)
        normed = (total * lax.rsqrt(spread + 1e-6) * gain[which : which + 1, :]).astype(BF16)
        for n in range(hidden.shape[1] // TILE):
            cols = slice(n * TILE, (n + 1) * TILE)
            u = jnp.dot(normed, wu[:, cols], preferred_element_type=F32)
            hidden[g * cells : (g + 1) * cells, cols] = gelu(u + bu[which : which + 1, cols]).astype(BF16)
        update = lax.dot_general(
            hidden[g * cells : (g + 1) * cells, :], wd[...], (((1,), (1,)), ((), ())), preferred_element_type=F32
        ).reshape(group, width, channels)
        result = (x_ref[part].astype(F32) + update).astype(BF16)
        out[part] = result
        at = pl.ds(g * group, group)
        stores.append(pltpu.make_async_copy(out.at[at], out_hbm.at[at], sem.at[16 + 2 * g]))
        stores[-1].start()
        if has_flux:
            flux = jnp.dot(result.reshape(cells, channels), fo[...], preferred_element_type=F32).astype(BF16)
            if split:
                for i in range(group):
                    piece = flux[i * width : (i + 1) * width].reshape(split, width // split, flux.shape[1])
                    surf[:, g * group + i] = piece
                store = pltpu.make_async_copy(surf.at[:, at], surf_hbm.at[:, at], sem.at[17 + 2 * g])
            else:
                surf[part] = flux.reshape(group, width, flux.shape[1])
                store = pltpu.make_async_copy(surf.at[at], surf_hbm.at[at], sem.at[17 + 2 * g])
            store.start()
            stores.append(store)
    for copy in ahead + stores:
        copy.wait()


def mix(which, x, known, halo, shared, flux_out=None, split=0, prefetch=()):
    kernel, gain, w_up, b_up, w_down = shared
    one, two, odd = halo
    rows, width, channels = x.shape
    has_flux = flux_out is not None
    cells = rows * width
    hidden = w_up.shape[-1]
    args = [near(x), near(known), near(one), near(two), odd]
    specs = [VMEM] * 4 + [pl.BlockSpec(memory_space=pltpu.SMEM)]
    far_args = [kernel, gain, w_up, b_up, w_down]
    out_shape = [jax.ShapeDtypeStruct((rows, width, channels), BF16)]
    out_specs = [ANY]
    plan = Plan(rows, TAPS)
    _, leaves = plan.split(range(PAD, PAD + rows))
    scratch = [
        pltpu.VMEM(kernel.shape, F32),
        pltpu.VMEM(gain.shape, F32),
        pltpu.VMEM(w_up.shape[1:], BF16),
        pltpu.VMEM(b_up.shape, F32),
        pltpu.VMEM(w_down.shape[1:], BF16),
        pltpu.VMEM((channels // LANES, len(leaves), width + 2 * SUB, LANES), F32),
        pltpu.VMEM((len(leaves), SUB, channels), F32),
        pltpu.VMEM((rows, width, channels), F32),
        pltpu.VMEM((cells, hidden), BF16),
        pltpu.VMEM((rows, width, channels), BF16),
        pltpu.SemaphoreType.DMA((32,)),
    ]
    if has_flux:
        far_args.append(flux_out)
        depth = flux_out.shape[1]
        shape = (split, rows, width // split, depth) if split else (rows, width, depth)
        out_shape.append(jax.ShapeDtypeStruct(shape, BF16))
        out_specs.append(ANY)
        scratch += [pltpu.VMEM(flux_out.shape, BF16), pltpu.VMEM(shape, BF16)]
    far_args += prefetch
    out_shape += [pltpu.VMEM(v.shape, v.dtype) for v in prefetch]
    out_specs += [VMEM] * len(prefetch)
    args += [far(v) for v in far_args]
    specs += [ANY] * len(far_args)
    return pl.pallas_call(
        functools.partial(mix_kernel, (which, has_flux, split, len(prefetch))),
        out_shape=out_shape,
        in_specs=specs,
        out_specs=out_specs,
        scratch_shapes=scratch,
        compiler_params=pltpu.CompilerParams(vmem_limit_bytes=LIMIT),
        cost_estimate=pl.CostEstimate(
            flops=4 * cells * channels * hidden, bytes_accessed=14 * cells * channels, transcendentals=cells * hidden
        ),
        name=f"mix{which}",
    )(*args)


def ocean_in_kernel(split, ocean_ref, moved_ref, mask_ref, fi_ref, out_ref, first_ref, last_ref):
    rows, width, channels = out_ref.shape
    mask = jnp.transpose(mask_ref[...].astype(F32))
    order = list(range(PAD)) + list(range(rows - PAD, rows)) + list(range(PAD, rows - PAD))
    for i in order:
        moved = moved_ref[:, i].reshape(width, fi_ref.shape[0]) if split else moved_ref[i]
        forcing = jnp.dot(moved, fi_ref[...], preferred_element_type=F32)
        value = (ocean_ref[i].astype(F32) + mask[:, i : i + 1] * forcing).astype(BF16)
        out_ref[i] = value
        if i < PAD:
            first_ref[i] = value
        if i >= rows - PAD:
            last_ref[i - rows + PAD] = value


def ocean_input(ocean, moved, mask, flux_in, split):
    rows, width, channels = ocean.shape
    shapes = [(rows, width, channels), (PAD, width, channels), (PAD, width, channels)]
    return pl.pallas_call(
        functools.partial(ocean_in_kernel, split),
        out_shape=[pltpu.VMEM(shape, BF16) for shape in shapes],
        in_specs=[VMEM] * 4,
        out_specs=[VMEM] * 3,
        compiler_params=pltpu.CompilerParams(vmem_limit_bytes=8 << 20),
        cost_estimate=pl.CostEstimate(
            flops=2 * rows * width * channels * flux_in.shape[0], bytes_accessed=8 * rows * width * channels, transcendentals=0
        ),
        name="ocean_in",
    )(near(ocean), near(moved), near(mask), near(flux_in))


def halos(first, last):
    size = lax.axis_size("band")
    odd = lax.axis_index("band") % 2
    inner = [(i, i ^ 1) for i in range(size)]
    outer = [(i, i + 1) for i in range(1, size - 1, 2)] + [(i + 1, i) for i in range(1, size - 1, 2)]
    one = lax.ppermute(jnp.where(odd == 1, first, last), "band", inner)
    two = lax.ppermute(jnp.where(odd == 1, last, first), "band", outer)
    return one, two, odd.astype(jnp.int32).reshape(1)


def per_device(
    atm_state,
    ocean_state,
    dw_kernel,
    norm_gain,
    w_up,
    b_up,
    w_down,
    flux_out,
    flux_in,
    partner,
    remap,
    land_mask,
):
    height, width, channels = atm_state.shape
    size = lax.axis_size("band")
    share = width // size
    split = size if share % SUB == 0 else 0
    band_rows = remap.shape[0] // partner.shape[0]
    indices = jnp.repeat(partner, band_rows) * band_rows + remap
    shared = (dw_kernel.transpose(1, 2, 0, 3), norm_gain, w_up, b_up, w_down)

    halo = halos(atm_state[:PAD], atm_state[-PAD:])
    known = early(0, atm_state, shared[0])
    atm_next, surface, ocean, mask, fi = mix(
        0, atm_state, known, halo, shared, flux_out, split, (ocean_state, land_mask, flux_in)
    )
    if not split:
        surface = surface.reshape(height, size, share, -1).transpose(1, 0, 2, 3)
    spread = lax.all_to_all(surface, "band", split_axis=0, concat_axis=0, tiled=True)
    picked = jnp.take(spread.reshape((size * height,) + spread.shape[2:]), indices, axis=0, mode="clip")
    moved = lax.all_to_all(picked.reshape(spread.shape), "band", split_axis=0, concat_axis=0, tiled=True)
    if not split:
        moved = moved.transpose(1, 0, 2, 3).reshape(height, width, -1)
    ocean_in, first, last = ocean_input(ocean, moved, mask, fi, split)
    halo = halos(first, last)
    known = early(1, ocean_in, shared[0])
    (ocean_next,) = mix(1, ocean_in, known, halo, shared)
    return (atm_next, ocean_next)


def solution(mesh):
    in_specs = (
        P(("ens", "band"), None, None),
        P(("ens", "band"), None, None),
        P(),
        P(),
        P(),
        P(),
        P(),
        P(),
        P(),
        P("ens"),
        P("ens"),
        P(("ens", "band"), None),
    )
    out_specs = (P(("ens", "band"), None, None), P(("ens", "band"), None, None))
    return jax.shard_map(
        per_device, mesh=mesh, in_specs=in_specs, out_specs=out_specs, check_vma=False
    )
```

```python
import functools

import jax
import jax.numpy as jnp
from jax import lax
from jax.experimental import pallas as pl
from jax.experimental.pallas import tpu as pltpu
from jax.sharding import PartitionSpec as P

LANES = 128
SUB = 8
TAPS = 7
PAD = TAPS // 2
TILE = 256
F32 = jnp.float32
BF16 = jnp.bfloat16
VMEM = pl.BlockSpec(memory_space=pltpu.VMEM)
ANY = pl.BlockSpec(memory_space=pl.ANY)
LIMIT = 24 << 20


def far(x):
    return pltpu.with_memory_space_constraint(x, pltpu.HBM)


def near(x):
    return pltpu.with_memory_space_constraint(x, pltpu.VMEM)


class Plan:
    def __init__(self, rows, taps):
        self.rows = rows
        self.z_ops, self.k_ops, self.leaves = [], [], []
        self.z_index, self.k_index = {}, {}
        zs = [self.z(("row", m)) for m in range(rows + taps - 1)]
        ks = [self.k(("tap", a)) for a in range(taps)]
        self.outs = self.fast(zs, ks, rows)

    def z(self, op):
        if op not in self.z_index:
            self.z_index[op] = len(self.z_ops)
            self.z_ops.append(op)
        return self.z_index[op]

    def k(self, op):
        if op not in self.k_index:
            self.k_index[op] = len(self.k_ops)
            self.k_ops.append(op)
        return self.k_index[op]

    def leaf(self, z, k):
        self.leaves.append((z, k))
        return ("leaf", len(self.leaves) - 1)

    def fast(self, zs, ks, count):
        if count % 2 or len(ks) == 1:
            outs = []
            for i in range(count):
                node = self.leaf(zs[i], ks[0])
                for j in range(1, len(ks)):
                    node = ("add", node, self.leaf(zs[i + j], ks[j]))
                outs.append(node)
            return outs
        half = count // 2
        even, odd, k0, k1 = zs[0::2], zs[1::2], ks[0::2], ks[1::2]
        both = [self.k(("add", k0[j], k1[j])) if j < len(k1) else k0[j] for j in range(len(k0))]
        need = half + len(k0) - 1
        first = self.fast(odd[:need], both, half)
        second = self.fast([self.z(("sub", even[n], odd[n])) for n in range(need)], k0, half)
        need = half + len(k1) - 1
        third = self.fast([self.z(("sub", even[n + 1], odd[n])) for n in range(need)], k1, half)
        outs = []
        for n in range(half):
            outs += [("add", first[n], second[n]), ("add", first[n], third[n])]
        return outs


def fill(load, rows, products, derived, width, lane_blocks):
    last = width // SUB - 1
    for block in range(width // SUB):
        for cb in range(lane_blocks):
            lons, lanes = slice(block * SUB, (block + 1) * SUB), slice(cb * LANES, (cb + 1) * LANES)
            for n, value in enumerate(rows(lambda m: load(m, lons, lanes).astype(F32))):
                derived[cb, n, (block + 1) * SUB : (block + 2) * SUB, :] = value
                if block == 0:
                    derived[cb, n, width + SUB : width + 2 * SUB, :] = value
                if block == last:
                    derived[cb, n, 0:SUB, :] = value


def fir(derived, weights, cb, z, n, start, wide):
    lanes = slice(cb * LANES, (cb + 1) * LANES)
    total = [None] * wide
    for b in range(TAPS):
        weight = jnp.broadcast_to(weights[n, b : b + 1, lanes], (SUB, LANES))
        for v in range(wide):
            term = weight * derived[cb, z, pl.ds(start + (SUB - PAD + b + v * SUB), SUB), :]
            total[v] = term if total[v] is None else total[v] + term
    return total


def own_rows(plan):
    def rows(load):
        values = {}

        def node(z):
            if z not in values:
                op = plan.z_ops[z]
                if op[0] == "row":
                    inside = PAD <= op[1] < PAD + plan.rows
                    values[z] = load(op[1] - PAD) if inside else None
                else:
                    left, right = node(op[1]), node(op[2])
                    values[z] = left if right is None else (-right if left is None else left - right)
            return values[z]

        return [node(z) for z, _ in plan.leaves]

    return rows


def tap_rows(kernel_ref, which, plan, weights):
    values = []
    for op in plan.k_ops:
        if op[0] == "tap":
            values.append(kernel_ref[op[1], :, which, :])
        else:
            values.append(values[op[1]] + values[op[2]])
    for n, (_, k) in enumerate(plan.leaves):
        weights[n, 0:TAPS, :] = values[k]


EDGE_PRODUCTS = ((3, 1, None), (0, 0, 1), (2, 2, None), (1, 2, 1), (0, 2, None))
EDGE_OUTS = ((0, 1, 2), (0, 3), (4,))


def gelu(u):
    half = 0.5 * u
    return half + half * jnp.tanh(u * (0.7978845608028654 + 0.035677408136300125 * (u * u)))


def expand(which, total, gain, wu, bu, hidden):
    center = jnp.mean(total, axis=-1, keepdims=True)
    total = total - center
    spread = jnp.mean(total * total, axis=-1, keepdims=True)
    normed = (total * lax.rsqrt(spread + 1e-6) * gain[which : which + 1, :]).astype(BF16)
    for n in range(hidden.shape[1] // TILE):
        cols = slice(n * TILE, (n + 1) * TILE)
        u = jnp.dot(normed, wu[:, cols], preferred_element_type=F32)
        hidden[:, cols] = gelu(u + bu[which : which + 1, cols]).astype(BF16)


def contract(split, base, hidden, x_ref, wd, out, flux_refs):
    count, width, channels = out.shape
    update = lax.dot_general(
        hidden[...], wd[...], (((1,), (1,)), ((), ())), preferred_element_type=F32
    )
    for n in range(count):
        out[n] = (x_ref[base + n].astype(F32) + update[n * width : (n + 1) * width]).astype(BF16)
    if flux_refs:
        fo, surf = flux_refs
        flux = jnp.dot(out[...].reshape(count * width, channels), fo[...], preferred_element_type=F32).astype(BF16)
        for n in range(count):
            row = flux[n * width : (n + 1) * width]
            if split:
                surf[:, n] = row.reshape(split, width // split, flux.shape[1])
            else:
                surf[n] = row


def surface_rows(split, ref, first, count):
    return ref.at[:, pl.ds(first, count)] if split else ref.at[pl.ds(first, count)]


def own_kernel(which, *refs):
    x_ref, kernel, *refs = refs
    number = (len(refs) - 4) // 2
    sources, acc_ref, targets = refs[:number], refs[number], refs[number + 1 : 2 * number + 1]
    derived, weights, sem = refs[2 * number + 1 :]
    rows, width, channels = x_ref.shape
    lane_blocks = channels // LANES
    plan = Plan(rows, TAPS)
    copies = [
        pltpu.make_async_copy(source.at[which] if len(source.shape) == 3 else source, target, sem.at[n])
        for n, (source, target) in enumerate(zip(sources, targets))
    ]
    for copy in copies:
        copy.start()
    fill(
        lambda m, lons, lanes: x_ref[m, lons, lanes], own_rows(plan), plan.leaves, derived, width, lane_blocks
    )
    tap_rows(kernel, which, plan, weights)
    wide = 2 if width % (2 * SUB) == 0 else 1
    for cb in range(lane_blocks):
        lanes = slice(cb * LANES, (cb + 1) * LANES)

        @pl.loop(0, width // (wide * SUB))
        def _(step):
            start = pl.multiple_of(step * (wide * SUB), wide * SUB)
            done = {}

            def value(node):
                if node not in done:
                    if node[0] == "add":
                        left, right = value(node[1]), value(node[2])
                        done[node] = [a + b for a, b in zip(left, right)]
                    else:
                        done[node] = fir(derived, weights, cb, node[1], node[1], start, wide)
                return done[node]

            for i, node in enumerate(plan.outs):
                for v, part in enumerate(value(node)):
                    acc_ref[i, pl.ds(start + v * SUB, SUB), lanes] = part

    for copy in copies:
        copy.wait()


def side_kernel(cfg, *refs):
    which, has_flux, split, first, prefetch = cfg
    refs = list(refs)
    x_ref, acc_ref, wu, wd, kernel, gain, bu, halo_ref = [refs.pop(0) for _ in range(8)]
    fo = refs.pop(0) if has_flux else None
    rows, width, channels = x_ref.shape
    middle = rows - 2 * PAD
    held = [refs.pop(0) for _ in range((1 + has_flux) * (not first))]
    odd_ref = refs.pop(0)
    sources = [refs.pop(0) for _ in range(prefetch)]
    surf = None
    if first:
        out = refs.pop(0)
        surf = refs.pop(0) if has_flux else None
        targets = [refs.pop(0) for _ in range(prefetch)]
        derived, weights, conv, hidden, sem = refs
    else:
        out_hbm = refs.pop(0)
        surf_hbm = refs.pop(0) if has_flux else None
        targets = [refs.pop(0) for _ in range(prefetch)]
        derived, weights, conv, hidden, sem, out = refs[:6]
        surf = refs[6] if has_flux else None
    lane_blocks = channels // LANES
    before = odd_ref[0] if first else 1 - odd_ref[0]
    count = PAD + middle if first else PAD
    base = (1 - before) * (rows - count)

    copies = [(source, target) for source, target in zip(sources, targets)]
    if not first:
        place = before * PAD
        copies.append((held[0], out_hbm.at[pl.ds(place, PAD + middle)]))
        if has_flux:
            copies.append((held[1], surface_rows(split, surf_hbm, place, PAD + middle)))
    copies = [pltpu.make_async_copy(a, b, sem.at[n]) for n, (a, b) in enumerate(copies)]
    for copy in copies:
        copy.start()

    def rows_of(load):
        d = [load(before * (PAD - 1 - j) + (1 - before) * j) for j in range(PAD)]
        return d + [d[0] + d[1]]

    def taps(j):
        return kernel[before * (PAD - 1 - j) + (1 - before) * (PAD + 1 + j), :, which, :]

    fill(lambda m, lons, lanes: halo_ref[m, lons, lanes], rows_of, EDGE_PRODUCTS, derived, width, lane_blocks)
    for n, (_, add, subtract) in enumerate(EDGE_PRODUCTS):
        weights[n, 0:TAPS, :] = taps(add) if subtract is None else taps(add) - taps(subtract)
    wide = 2 if width % (2 * SUB) == 0 else 1
    for cb in range(lane_blocks):
        lanes = slice(cb * LANES, (cb + 1) * LANES)

        @pl.loop(0, width // (wide * SUB))
        def _(step):
            start = pl.multiple_of(step * (wide * SUB), wide * SUB)
            done = {}
            for j, products in enumerate(EDGE_OUTS):
                row = before * j + (1 - before) * (rows - 1 - j)
                total = [acc_ref[row, pl.ds(start + v * SUB, SUB), lanes] for v in range(wide)]
                for n in products:
                    if n not in done:
                        done[n] = fir(derived, weights, cb, EDGE_PRODUCTS[n][0], n, start, wide)
                    total = [a + b for a, b in zip(total, done[n])]
                for v in range(wide):
                    conv[row - base, pl.ds(start + v * SUB, SUB), lanes] = total[v]

    if first:
        for n in range(middle):
            conv[before * PAD + n] = acc_ref[PAD + n]
    expand(which, conv[...].reshape(count * width, channels), gain, wu, bu, hidden)
    contract(split, base, hidden, x_ref, wd, out, (fo, surf) if has_flux else None)
    if not first:
        pairs = [(out, out_hbm.at[pl.ds(base, PAD)])]
        if has_flux:
            pairs.append((surf, surface_rows(split, surf_hbm, base, PAD)))
        for a, b in pairs:
            copies.append(pltpu.make_async_copy(a, b, sem.at[len(copies)]))
            copies[-1].start()
    for copy in copies:
        copy.wait()


def mix(which, x, halo, shared, small, flux_out=None, split=0, prefetch=()):
    w_up, w_down = shared
    kernel, gain, b_up = small
    one, two, odd = halo
    rows, width, channels = x.shape
    has_flux = flux_out is not None
    hidden = w_up.shape[-1]
    blocks = channels // LANES
    middle = rows - 2 * PAD
    smem = pl.BlockSpec(memory_space=pltpu.SMEM)

    def piece(count):
        return (split, count, width // split, depth) if split else (count, width, depth)

    def cost(count):
        cells = count * width
        return pl.CostEstimate(
            flops=4 * cells * channels * hidden, bytes_accessed=14 * cells * channels, transcendentals=cells * hidden
        )

    model = [w_up, w_down]
    loaded = [pltpu.VMEM(w_up.shape[1:], BF16), pltpu.VMEM(w_down.shape[1:], BF16)]
    if has_flux:
        depth = flux_out.shape[1]
        model.append(flux_out)
        loaded.append(pltpu.VMEM(flux_out.shape, BF16))
    leaves = len(Plan(rows, TAPS).leaves)
    acc, *loaded = pl.pallas_call(
        functools.partial(own_kernel, which),
        out_shape=[pltpu.VMEM((rows, width, channels), F32)] + loaded,
        in_specs=[VMEM] * 2 + [ANY] * len(model),
        out_specs=[VMEM] * (1 + len(loaded)),
        scratch_shapes=[
            pltpu.VMEM((blocks, leaves, width + 2 * SUB, LANES), F32),
            pltpu.VMEM((leaves, SUB, channels), F32),
            pltpu.SemaphoreType.DMA((4,)),
        ],
        compiler_params=pltpu.CompilerParams(vmem_limit_bytes=16 << 20),
        cost_estimate=pl.CostEstimate(
            flops=60 * rows * width * channels, bytes_accessed=8 * rows * width * channels, transcendentals=0
        ),
        name=f"own{which}",
    )(near(x), near(kernel), *[far(v) for v in model])

    def side(first, halo_rows, held, out_shape, prefetch):
        count = PAD + middle if first else PAD
        close = [x, acc, *loaded[:2], kernel, gain, b_up, halo_rows] + loaded[2:] + held
        scratch = [
            pltpu.VMEM((blocks, PAD + 1, width + 2 * SUB, LANES), F32),
            pltpu.VMEM((len(EDGE_PRODUCTS), SUB, channels), F32),
            pltpu.VMEM((count, width, channels), F32),
            pltpu.VMEM((count * width, hidden), BF16),
            pltpu.SemaphoreType.DMA((16,)),
        ]
        if not first:
            scratch.append(pltpu.VMEM((count, width, channels), BF16))
            if has_flux:
                scratch.append(pltpu.VMEM(piece(count), BF16))
        return pl.pallas_call(
            functools.partial(side_kernel, (which, has_flux, split, first, len(prefetch))),
            out_shape=out_shape + [pltpu.VMEM(v.shape, v.dtype) for v in prefetch],
            in_specs=[VMEM] * len(close) + [smem] + [ANY] * len(prefetch),
            out_specs=[VMEM if first else ANY] * len(out_shape) + [VMEM] * len(prefetch),
            scratch_shapes=scratch,
            compiler_params=pltpu.CompilerParams(vmem_limit_bytes=LIMIT),
            cost_estimate=cost(count),
            name=f"side{which}_{int(first)}",
        )(*[near(v) for v in close], odd, *[far(v) for v in prefetch])

    held_shape = [pltpu.VMEM((PAD + middle, width, channels), BF16)]
    out_shape = [jax.ShapeDtypeStruct((rows, width, channels), BF16)]
    if has_flux:
        held_shape.append(pltpu.VMEM(piece(PAD + middle), BF16))
        out_shape.append(jax.ShapeDtypeStruct(piece(rows), BF16))
    held = side(True, one, [], held_shape, ())
    return side(False, two, list(held), out_shape, prefetch)


def stage_kernel(number, x_hbm, odd_ref, *refs):
    sources, (x_ref, one_ref, two_ref), targets, sem = refs[:number], refs[number : number + 3], refs[number + 3 : -1], refs[-1]
    last = x_hbm.shape[0] - PAD
    odd = odd_ref[0]
    pairs = [
        (x_hbm.at[pl.ds(odd * last, PAD)], two_ref),
        (x_hbm.at[pl.ds((1 - odd) * last, PAD)], one_ref),
        (x_hbm, x_ref),
        *zip(sources, targets),
    ]
    copies = [pltpu.make_async_copy(a, b, sem.at[n]) for n, (a, b) in enumerate(pairs)]
    for copy in copies:
        copy.start()
    for copy in copies:
        copy.wait()


def stage(x, odd, small):
    edge = pltpu.VMEM((PAD,) + x.shape[1:], x.dtype)
    return pl.pallas_call(
        functools.partial(stage_kernel, len(small)),
        out_shape=[pltpu.VMEM(x.shape, x.dtype), edge, edge] + [pltpu.VMEM(v.shape, v.dtype) for v in small],
        in_specs=[ANY, pl.BlockSpec(memory_space=pltpu.SMEM)] + [ANY] * len(small),
        out_specs=[VMEM] * (3 + len(small)),
        scratch_shapes=[pltpu.SemaphoreType.DMA((3 + len(small),))],
        compiler_params=pltpu.CompilerParams(vmem_limit_bytes=1 << 20),
        name="stage",
    )(far(x), odd, *[far(v) for v in small])


def ocean_in_kernel(split, ocean_ref, moved_ref, mask_ref, fi_ref, odd_ref, out_ref, edges_ref):
    rows, width, channels = out_ref.shape
    mask = jnp.transpose(mask_ref[...].astype(F32))
    order = list(range(PAD)) + list(range(rows - PAD, rows)) + list(range(PAD, rows - PAD))
    for i in order:
        moved = moved_ref[:, i].reshape(width, fi_ref.shape[0]) if split else moved_ref[i]
        forcing = jnp.dot(moved, fi_ref[...], preferred_element_type=F32)
        value = (ocean_ref[i].astype(F32) + mask[:, i : i + 1] * forcing).astype(BF16)
        out_ref[i] = value
        if i < PAD:
            edges_ref[1 - odd_ref[0], i] = value
        if i >= rows - PAD:
            edges_ref[odd_ref[0], i - rows + PAD] = value


def ocean_input(ocean, moved, mask, flux_in, odd, split):
    rows, width, channels = ocean.shape
    return pl.pallas_call(
        functools.partial(ocean_in_kernel, split),
        out_shape=[pltpu.VMEM((rows, width, channels), BF16), pltpu.VMEM((2, PAD, width, channels), BF16)],
        in_specs=[VMEM] * 4 + [pl.BlockSpec(memory_space=pltpu.SMEM)],
        out_specs=[VMEM] * 2,
        compiler_params=pltpu.CompilerParams(vmem_limit_bytes=8 << 20),
        cost_estimate=pl.CostEstimate(
            flops=2 * rows * width * channels * flux_in.shape[0], bytes_accessed=8 * rows * width * channels, transcendentals=0
        ),
        name="ocean_in",
    )(near(ocean), near(moved), near(mask), near(flux_in), odd)


def halos(one, two):
    size = lax.axis_size("band")
    inner = [(i, i ^ 1) for i in range(size)]
    outer = [(i, i + 1) for i in range(1, size - 1, 2)] + [(i + 1, i) for i in range(1, size - 1, 2)]
    return lax.ppermute(one, "band", inner), lax.ppermute(two, "band", outer)


def per_device(
    atm_state,
    ocean_state,
    dw_kernel,
    norm_gain,
    w_up,
    b_up,
    w_down,
    flux_out,
    flux_in,
    partner,
    remap,
    land_mask,
):
    height, width, channels = atm_state.shape
    size = lax.axis_size("band")
    share = width // size
    split = size if share % SUB == 0 else 0
    band_rows = remap.shape[0] // partner.shape[0]
    indices = jnp.repeat(partner, band_rows) * band_rows + remap
    shared = (w_up, w_down)

    odd = (lax.axis_index("band") % 2).astype(jnp.int32).reshape(1)

    atm, one, two, *small = stage(atm_state, odd, [dw_kernel.transpose(1, 2, 0, 3), norm_gain, b_up])
    halo = (*halos(one, two), odd)
    atm_next, surface, ocean, mask, fi = mix(
        0, atm, halo, shared, small, flux_out, split, (ocean_state, land_mask, flux_in)
    )
    if not split:
        surface = surface.reshape(height, size, share, -1).transpose(1, 0, 2, 3)
    spread = lax.all_to_all(surface, "band", split_axis=0, concat_axis=0, tiled=True)
    picked = jnp.take(spread.reshape((size * height,) + spread.shape[2:]), indices, axis=0, mode="clip")
    moved = lax.all_to_all(picked.reshape(spread.shape), "band", split_axis=0, concat_axis=0, tiled=True)
    if not split:
        moved = moved.transpose(1, 0, 2, 3).reshape(height, width, -1)
    ocean_in, edges = ocean_input(ocean, moved, mask, fi, odd, split)
    halo = (*halos(edges[0], edges[1]), odd)
    (ocean_next,) = mix(1, ocean_in, halo, shared, small)
    return (atm_next, ocean_next)


def solution(mesh):
    in_specs = (
        P(("ens", "band"), None, None),
        P(("ens", "band"), None, None),
        P(),
        P(),
        P(),
        P(),
        P(),
        P(),
        P(),
        P("ens"),
        P("ens"),
        P(("ens", "band"), None),
    )
    out_specs = (P(("ens", "band"), None, None), P(("ens", "band"), None, None))
    return jax.shard_map(
        per_device, mesh=mesh, in_specs=in_specs, out_specs=out_specs, check_vma=False
    )
```

```python
import functools

import jax
import jax.numpy as jnp
from jax import lax
from jax.experimental import pallas as pl
from jax.experimental.pallas import tpu as pltpu
from jax.sharding import PartitionSpec as P


LANES = 128
SUB = 8
TAPS = 7
PAD = TAPS // 2
TILE = 256
F32 = jnp.float32
BF16 = jnp.bfloat16
VMEM = pl.BlockSpec(memory_space=pltpu.VMEM)
ANY = pl.BlockSpec(memory_space=pl.ANY)
LIMIT = 24 << 20


def parity():
    return lax.axis_index("band") % 2


def far(x):
    return pltpu.with_memory_space_constraint(x, pltpu.HBM)


def near(x):
    return pltpu.with_memory_space_constraint(x, pltpu.VMEM)


class Plan:
    def __init__(self, rows, taps):
        self.rows = rows
        self.z_ops, self.k_ops, self.leaves = [], [], []
        self.z_index, self.k_index = {}, {}
        zs = [self.z(("row", m)) for m in range(rows + taps - 1)]
        ks = [self.k(("tap", a)) for a in range(taps)]
        self.outs = self.fast(zs, ks, rows)

    def z(self, op):
        if op not in self.z_index:
            self.z_index[op] = len(self.z_ops)
            self.z_ops.append(op)
        return self.z_index[op]

    def k(self, op):
        if op not in self.k_index:
            self.k_index[op] = len(self.k_ops)
            self.k_ops.append(op)
        return self.k_index[op]

    def leaf(self, z, k):
        self.leaves.append((z, k))
        return ("leaf", len(self.leaves) - 1)

    def fast(self, zs, ks, count):
        if count % 2 or len(ks) == 1:
            outs = []
            for i in range(count):
                node = self.leaf(zs[i], ks[0])
                for j in range(1, len(ks)):
                    node = ("add", node, self.leaf(zs[i + j], ks[j]))
                outs.append(node)
            return outs
        half = count // 2
        even, odd, k0, k1 = zs[0::2], zs[1::2], ks[0::2], ks[1::2]
        both = [self.k(("add", k0[j], k1[j])) if j < len(k1) else k0[j] for j in range(len(k0))]
        need = half + len(k0) - 1
        first = self.fast(odd[:need], both, half)
        second = self.fast([self.z(("sub", even[n], odd[n])) for n in range(need)], k0, half)
        need = half + len(k1) - 1
        third = self.fast([self.z(("sub", even[n + 1], odd[n])) for n in range(need)], k1, half)
        outs = []
        for n in range(half):
            outs += [("add", first[n], second[n]), ("add", first[n], third[n])]
        return outs


def fill(load, rows, derived, width, lane_blocks):
    last = width // SUB - 1
    for block in range(width // SUB):
        for cb in range(lane_blocks):
            lons, lanes = slice(block * SUB, (block + 1) * SUB), slice(cb * LANES, (cb + 1) * LANES)
            for n, value in enumerate(rows(lambda m: load(m, lons, lanes).astype(F32))):
                derived[cb, n, (block + 1) * SUB : (block + 2) * SUB, :] = value
                if block == 0:
                    derived[cb, n, width + SUB : width + 2 * SUB, :] = value
                if block == last:
                    derived[cb, n, 0:SUB, :] = value


def fir(derived, weights, cb, z, n, start, wide):
    lanes = slice(cb * LANES, (cb + 1) * LANES)
    total = [None] * wide
    for b in range(TAPS):
        weight = jnp.broadcast_to(weights[n, b : b + 1, lanes], (SUB, LANES))
        for v in range(wide):
            term = weight * derived[cb, z, pl.ds(start + (SUB - PAD + b + v * SUB), SUB), :]
            total[v] = term if total[v] is None else total[v] + term
    return total


def own_rows(plan):
    def rows(load):
        values = {}

        def node(z):
            if z not in values:
                op = plan.z_ops[z]
                if op[0] == "row":
                    inside = PAD <= op[1] < PAD + plan.rows
                    values[z] = load(op[1] - PAD) if inside else None
                else:
                    left, right = node(op[1]), node(op[2])
                    values[z] = left if right is None else (-right if left is None else left - right)
            return values[z]

        return [node(z) for z, _ in plan.leaves]

    return rows


def tap_rows(kernel_ref, which, plan, weights):
    values = []
    for op in plan.k_ops:
        if op[0] == "tap":
            values.append(kernel_ref[op[1], :, which, :])
        else:
            values.append(values[op[1]] + values[op[2]])
    for n, (_, k) in enumerate(plan.leaves):
        weights[n, 0:TAPS, :] = values[k]


EDGE_PRODUCTS = ((3, 1, None), (0, 0, 1), (2, 2, None), (1, 2, 1), (0, 2, None))
EDGE_OUTS = ((0, 1, 2), (0, 3), (4,))


def gelu(u):
    half = 0.5 * u
    return half + half * jnp.tanh(u * (0.7978845608028654 + 0.035677408136300125 * (u * u)))


def expand(which, total, gain, wu, bu, hidden):
    center = jnp.mean(total, axis=-1, keepdims=True)
    total = total - center
    spread = jnp.mean(total * total, axis=-1, keepdims=True)
    normed = (total * lax.rsqrt(spread + 1e-6) * gain[which : which + 1, :]).astype(BF16)
    for n in range(hidden.shape[1] // TILE):
        cols = slice(n * TILE, (n + 1) * TILE)
        u = jnp.dot(normed, wu[:, cols], preferred_element_type=F32)
        hidden[:, cols] = gelu(u + bu[which : which + 1, cols]).astype(BF16)


def contract(split, base, hidden, x_ref, wd, out, begin, size, flux_refs):
    count, width, channels = out.shape
    cols = slice(begin, begin + size)
    update = lax.dot_general(
        hidden[...], wd[cols, :], (((1,), (1,)), ((), ())), preferred_element_type=F32
    )
    for n in range(count):
        state = x_ref[base + n, :, cols].astype(F32)
        out[n, :, cols] = (state + update[n * width : (n + 1) * width]).astype(BF16)
    if flux_refs:
        fo, surf = flux_refs
        flux = jnp.dot(out[...].reshape(count * width, channels), fo[...], preferred_element_type=F32).astype(BF16)
        for n in range(count):
            row = flux[n * width : (n + 1) * width]
            if split:
                surf[:, n] = row.reshape(split, width // split, flux.shape[1])
            else:
                surf[n] = row


def surface_rows(split, ref, first, count):
    return ref.at[:, pl.ds(first, count)] if split else ref.at[pl.ds(first, count)]


def own_kernel(which, *refs):
    x_ref, kernel, *refs = refs
    number = (len(refs) - 4) // 2
    sources, acc_ref, targets = refs[:number], refs[number], refs[number + 1 : 2 * number + 1]
    derived, weights, sem = refs[2 * number + 1 :]
    rows, width, channels = x_ref.shape
    lane_blocks = channels // LANES
    plan = Plan(rows, TAPS)
    copies = [
        pltpu.make_async_copy(source.at[which] if len(source.shape) > len(target.shape) else source, target, sem.at[n])
        for n, (source, target) in enumerate(zip(sources, targets))
    ]
    for copy in copies:
        copy.start()
    fill(lambda m, lons, lanes: x_ref[m, lons, lanes], own_rows(plan), derived, width, lane_blocks)
    tap_rows(kernel, which, plan, weights)
    wide = 2 if width % (2 * SUB) == 0 else 1
    for cb in range(lane_blocks):
        lanes = slice(cb * LANES, (cb + 1) * LANES)

        @pl.loop(0, width // (wide * SUB))
        def _(step):
            start = pl.multiple_of(step * (wide * SUB), wide * SUB)
            done = {}

            def value(node):
                if node not in done:
                    if node[0] == "add":
                        left, right = value(node[1]), value(node[2])
                        done[node] = [a + b for a, b in zip(left, right)]
                    else:
                        done[node] = fir(derived, weights, cb, node[1], node[1], start, wide)
                return done[node]

            for i, node in enumerate(plan.outs):
                for v, part in enumerate(value(node)):
                    acc_ref[i, pl.ds(start + v * SUB, SUB), lanes] = part

    for copy in copies:
        copy.wait()


def side_kernel(cfg, *refs):
    which, has_flux, split, first, prefetch = cfg
    refs = list(refs)
    x_ref, acc_ref, wu, wd, kernel, gain, bu, halo_ref = [refs.pop(0) for _ in range(8)]
    fo = refs.pop(0) if has_flux else None
    rows, width, channels = x_ref.shape
    middle = rows - 2 * PAD
    held = [refs.pop(0) for _ in range((1 + has_flux) * (not first))]
    sources = [refs.pop(0) for _ in range(prefetch)]
    surf = None
    if first:
        out = refs.pop(0)
        surf = refs.pop(0) if has_flux else None
        targets = [refs.pop(0) for _ in range(prefetch)]
        derived, weights, conv, hidden, sem = refs
    else:
        out_all = refs.pop(0)
        surf_all = refs.pop(0) if has_flux else None
        targets = [refs.pop(0) for _ in range(prefetch)]
        derived, weights, conv, hidden, sem, out = refs if not has_flux else (*refs, None)
    lane_blocks = channels // LANES
    before = parity() if first else 1 - parity()
    count = PAD + middle if first else PAD
    base = (1 - before) * (rows - count)

    copies = [(source, target) for source, target in zip(sources, targets)]
    if not first:
        place = before * PAD
        copies.append((held[0], out_all.at[pl.ds(place, PAD + middle)]))
        if has_flux:
            out = out_all.at[pl.ds(base, PAD)]
            copies.append((held[1], surface_rows(split, surf_all, place, PAD + middle)))
            surf = surface_rows(split, surf_all, base, PAD)
    copies = [pltpu.make_async_copy(a, b, sem.at[n]) for n, (a, b) in enumerate(copies)]
    for copy in copies:
        copy.start()

    def rows_of(load):
        d = [load(before * (PAD - 1 - j) + (1 - before) * j) for j in range(PAD)]
        return d + [d[0] + d[1]]

    def taps(j):
        return kernel[before * (PAD - 1 - j) + (1 - before) * (PAD + 1 + j), :, which, :]

    fill(lambda m, lons, lanes: halo_ref[m, lons, lanes], rows_of, derived, width, lane_blocks)
    for n, (_, add, subtract) in enumerate(EDGE_PRODUCTS):
        weights[n, 0:TAPS, :] = taps(add) if subtract is None else taps(add) - taps(subtract)
    wide = 2 if width % (2 * SUB) == 0 else 1
    for cb in range(lane_blocks):
        lanes = slice(cb * LANES, (cb + 1) * LANES)

        @pl.loop(0, width // (wide * SUB))
        def _(step):
            start = pl.multiple_of(step * (wide * SUB), wide * SUB)
            done = {}
            for j, products in enumerate(EDGE_OUTS):
                row = before * j + (1 - before) * (rows - 1 - j)
                total = [acc_ref[row, pl.ds(start + v * SUB, SUB), lanes] for v in range(wide)]
                for n in products:
                    if n not in done:
                        done[n] = fir(derived, weights, cb, EDGE_PRODUCTS[n][0], n, start, wide)
                    total = [a + b for a, b in zip(total, done[n])]
                for v in range(wide):
                    conv[row - base, pl.ds(start + v * SUB, SUB), lanes] = total[v]

    if first:
        for n in range(middle):
            conv[before * PAD + n] = acc_ref[PAD + n]
    expand(which, conv[...].reshape(count * width, channels), gain, wu, bu, hidden)
    if has_flux or first:
        contract(split, base, hidden, x_ref, wd, out, 0, channels, (fo, surf) if has_flux else None)
    else:
        for begin in range(0, channels, TILE):
            size = min(TILE, channels - begin)
            contract(split, base, hidden, x_ref, wd, out, begin, size, None)
            cols = pl.ds(begin, size)
            copies.append(
                pltpu.make_async_copy(
                    out.at[:, :, cols], out_all.at[pl.ds(base, PAD), :, cols], sem.at[len(copies)]
                )
            )
            copies[-1].start()
    for copy in copies:
        copy.wait()


def mix(which, x, halo, shared, small, flux_out=None, split=0, prefetch=(), flush=None):
    w_up, w_down = shared
    kernel, gain, b_up = small
    one, two = halo
    rows, width, channels = x.shape
    has_flux = flux_out is not None
    hidden = w_up.shape[-1]
    blocks = channels // LANES
    middle = rows - 2 * PAD

    def piece(count):
        return (split, count, width // split, depth) if split else (count, width, depth)

    def cost(count):
        cells = count * width
        return pl.CostEstimate(
            flops=4 * cells * channels * hidden, bytes_accessed=14 * cells * channels, transcendentals=cells * hidden
        )

    model = [w_up, w_down]
    loaded = [pltpu.VMEM(w_up.shape[1:], BF16), pltpu.VMEM(w_down.shape[1:], BF16)]
    if has_flux:
        depth = flux_out.shape[1]
        model.append(flux_out)
        loaded.append(pltpu.VMEM(flux_out.shape, BF16))
    leaves = len(Plan(rows, TAPS).leaves)
    out_specs = [VMEM] * (1 + len(loaded))
    in_specs = [VMEM] * 2 + [ANY] * len(model)
    model = [far(v) for v in model]
    if flush is not None:
        model.append(near(flush))
        in_specs.append(VMEM)
        loaded.append(jax.ShapeDtypeStruct(flush.shape, flush.dtype))
        out_specs.append(ANY)
    acc, *loaded = pl.pallas_call(
        functools.partial(own_kernel, which),
        out_shape=[pltpu.VMEM((rows, width, channels), F32)] + loaded,
        in_specs=in_specs,
        out_specs=out_specs,
        scratch_shapes=[
            pltpu.VMEM((blocks, leaves, width + 2 * SUB, LANES), F32),
            pltpu.VMEM((leaves, SUB, channels), F32),
            pltpu.SemaphoreType.DMA((4,)),
        ],
        compiler_params=pltpu.CompilerParams(vmem_limit_bytes=16 << 20),
        cost_estimate=pl.CostEstimate(
            flops=60 * rows * width * channels, bytes_accessed=8 * rows * width * channels, transcendentals=0
        ),
    )(near(x), near(kernel), *model)
    flushed = [loaded.pop()] if flush is not None else []

    def side(first, halo_rows, held, out_shape, prefetch):
        count = PAD + middle if first else PAD
        close = [x, acc, *loaded[:2], kernel, gain, b_up, halo_rows] + loaded[2:] + held
        scratch = [
            pltpu.VMEM((blocks, PAD + 1, width + 2 * SUB, LANES), F32),
            pltpu.VMEM((len(EDGE_PRODUCTS), SUB, channels), F32),
            pltpu.VMEM((count, width, channels), F32),
            pltpu.VMEM((count * width, hidden), BF16),
            pltpu.SemaphoreType.DMA((16,)),
        ]
        if not first:
            scratch += [] if has_flux else [pltpu.VMEM((count, width, channels), BF16)]
        return pl.pallas_call(
            functools.partial(side_kernel, (which, has_flux, split, first, len(prefetch))),
            out_shape=out_shape + [pltpu.VMEM(v.shape, v.dtype) for v in prefetch],
            in_specs=[VMEM] * len(close) + [ANY] * len(prefetch),
            out_specs=[VMEM if first or has_flux else ANY] + [VMEM] * (len(out_shape) - 1 + len(prefetch)),
            scratch_shapes=scratch,
            compiler_params=pltpu.CompilerParams(vmem_limit_bytes=LIMIT),
            cost_estimate=cost(count),
        )(*[near(v) for v in close], *[far(v) for v in prefetch])

    held_shape = [pltpu.VMEM((PAD + middle, width, channels), BF16)]
    full = pltpu.VMEM if has_flux else jax.ShapeDtypeStruct
    out_shape = [full((rows, width, channels), BF16)]
    if has_flux:
        held_shape.append(pltpu.VMEM(piece(PAD + middle), BF16))
        out_shape.append(pltpu.VMEM(piece(rows), BF16))
    held = side(True, one, [], held_shape, ())
    return [*side(False, two, list(held), out_shape, prefetch), *flushed]


def stage_kernel(number, x_hbm, *refs):
    sources, (x_ref, one_ref, two_ref), targets, sem = refs[:number], refs[number : number + 3], refs[number + 3 : -1], refs[-1]
    last = x_hbm.shape[0] - PAD
    odd = parity()
    pairs = [
        (x_hbm.at[pl.ds(odd * last, PAD)], two_ref),
        (x_hbm.at[pl.ds((1 - odd) * last, PAD)], one_ref),
        (x_hbm, x_ref),
        *zip(sources, targets),
    ]
    copies = [pltpu.make_async_copy(a, b, sem.at[n]) for n, (a, b) in enumerate(pairs)]
    for copy in copies:
        copy.start()
    for copy in copies:
        copy.wait()


def stage(x, small):
    edge = pltpu.VMEM((PAD,) + x.shape[1:], x.dtype)
    return pl.pallas_call(
        functools.partial(stage_kernel, len(small)),
        out_shape=[pltpu.VMEM(x.shape, x.dtype), edge, edge] + [pltpu.VMEM(v.shape, v.dtype) for v in small],
        in_specs=[ANY] * (1 + len(small)),
        out_specs=[VMEM] * (3 + len(small)),
        scratch_shapes=[pltpu.SemaphoreType.DMA((3 + len(small),))],
        compiler_params=pltpu.CompilerParams(vmem_limit_bytes=1 << 20),
        name="stage",
    )(far(x), *[far(v) for v in small])


def pick_kernel(partner_ref, remap_ref, x_ref, out_ref):
    bands, rows = out_ref.shape[:2]
    for o in range(bands):
        for r in range(rows):
            out_ref[o, r] = x_ref[partner_ref[o], remap_ref[o * rows + r]]


def pick_rows(x, partner, remap):
    if x.shape[2] % SUB:
        height = x.shape[1]
        indices = jnp.repeat(partner, height) * height + remap
        return jnp.take(x.reshape((-1,) + x.shape[2:]), indices, axis=0, mode="clip").reshape(x.shape)
    smem = pl.BlockSpec(memory_space=pltpu.SMEM)
    return pl.pallas_call(
        pick_kernel,
        out_shape=pltpu.VMEM(x.shape, x.dtype),
        in_specs=[smem, smem, VMEM],
        out_specs=VMEM,
        compiler_params=pltpu.CompilerParams(vmem_limit_bytes=1 << 20),
        name="pick",
    )(*[pltpu.with_memory_space_constraint(v, pltpu.SMEM) for v in (partner, remap)], near(x))


def ocean_in_kernel(split, ocean_ref, moved_ref, mask_ref, fi_ref, out_ref, edges_ref):
    rows, width, _ = out_ref.shape
    odd = parity()
    mask = jnp.transpose(mask_ref[...].astype(F32))
    order = list(range(PAD)) + list(range(rows - PAD, rows)) + list(range(PAD, rows - PAD))
    for i in order:
        moved = moved_ref[:, i].reshape(width, fi_ref.shape[0]) if split else moved_ref[i]
        forcing = jnp.dot(moved, fi_ref[...], preferred_element_type=F32)
        value = (ocean_ref[i].astype(F32) + mask[:, i : i + 1] * forcing).astype(BF16)
        out_ref[i] = value
        if i < PAD:
            edges_ref[1 - odd, i] = value
        if i >= rows - PAD:
            edges_ref[odd, i - rows + PAD] = value


def ocean_input(ocean, moved, mask, flux_in, split):
    rows, width, channels = ocean.shape
    return pl.pallas_call(
        functools.partial(ocean_in_kernel, split),
        out_shape=[pltpu.VMEM((rows, width, channels), BF16), pltpu.VMEM((2, PAD, width, channels), BF16)],
        in_specs=[VMEM] * 4,
        out_specs=[VMEM] * 2,
        compiler_params=pltpu.CompilerParams(vmem_limit_bytes=8 << 20),
        cost_estimate=pl.CostEstimate(
            flops=2 * rows * width * channels * flux_in.shape[0], bytes_accessed=8 * rows * width * channels, transcendentals=0
        ),
        name="ocean_in",
    )(near(ocean), near(moved), near(mask), near(flux_in))


def halos(one, two):
    size = lax.axis_size("band")
    inner = [(i, i ^ 1) for i in range(size)]
    outer = [(i, i + 1) for i in range(1, size - 1, 2)] + [(i + 1, i) for i in range(1, size - 1, 2)]
    two = lax.ppermute(two, "band", outer)
    one = lax.ppermute(one, "band", inner)
    return one, two


def per_device(
    atm_state,
    ocean_state,
    dw_kernel,
    norm_gain,
    w_up,
    b_up,
    w_down,
    flux_out,
    flux_in,
    partner,
    remap,
    land_mask,
):
    height, width, _ = atm_state.shape
    size = lax.axis_size("band")
    share = width // size
    split = size if share % SUB == 0 else 0
    shared = (w_up, w_down)

    atm, one, two, *small = stage(atm_state, [dw_kernel.transpose(1, 2, 0, 3), norm_gain, b_up])
    halo = halos(one, two)
    atm_next, surface, ocean, mask, fi = mix(
        0, atm, halo, shared, small, flux_out, split, (ocean_state, land_mask, flux_in)
    )
    if not split:
        surface = surface.reshape(height, size, share, -1).transpose(1, 0, 2, 3)
    spread = lax.all_to_all(surface, "band", split_axis=0, concat_axis=0, tiled=True)
    picked = pick_rows(spread, partner, remap)
    moved = lax.all_to_all(picked, "band", split_axis=0, concat_axis=0, tiled=True)
    if not split:
        moved = moved.transpose(1, 0, 2, 3).reshape(height, width, -1)
    ocean_in, edges = ocean_input(ocean, moved, mask, fi, split)
    halo = halos(edges[0], edges[1])
    ocean_next, atm_next = mix(1, ocean_in, halo, shared, small, flush=atm_next)
    return (atm_next, ocean_next)


def solution(mesh):
    in_specs = (
        P(("ens", "band"), None, None),
        P(("ens", "band"), None, None),
        P(),
        P(),
        P(),
        P(),
        P(),
        P(),
        P(),
        P("ens"),
        P("ens"),
        P(("ens", "band"), None),
    )
    out_specs = (P(("ens", "band"), None, None), P(("ens", "band"), None, None))

    return jax.shard_map(per_device, mesh=mesh, in_specs=in_specs, out_specs=out_specs, check_vma=False)
```

```python
import functools

import jax
import jax.numpy as jnp
from jax import lax
from jax.experimental import pallas as pl
from jax.experimental.pallas import tpu as pltpu
from jax.sharding import PartitionSpec as P


LANES = 128
SUB = 8
TAPS = 7
PAD = TAPS // 2
TILE = 256
F32 = jnp.float32
BF16 = jnp.bfloat16
VMEM = pl.BlockSpec(memory_space=pltpu.VMEM)
ANY = pl.BlockSpec(memory_space=pl.ANY)
LIMIT = 24 << 20


def parity():
    return lax.axis_index("band") % 2


def far(x):
    return pltpu.with_memory_space_constraint(x, pltpu.HBM)


def near(x):
    return pltpu.with_memory_space_constraint(x, pltpu.VMEM)


class Plan:
    def __init__(self, rows, taps):
        self.rows = rows
        self.z_ops, self.k_ops, self.leaves = [], [], []
        self.z_index, self.k_index = {}, {}
        zs = [self.z(("row", m)) for m in range(rows + taps - 1)]
        ks = [self.k(("tap", a)) for a in range(taps)]
        self.outs = self.fast(zs, ks, rows)

    def z(self, op):
        if op not in self.z_index:
            self.z_index[op] = len(self.z_ops)
            self.z_ops.append(op)
        return self.z_index[op]

    def k(self, op):
        if op not in self.k_index:
            self.k_index[op] = len(self.k_ops)
            self.k_ops.append(op)
        return self.k_index[op]

    def leaf(self, z, k):
        self.leaves.append((z, k))
        return ("leaf", len(self.leaves) - 1)

    def fast(self, zs, ks, count):
        if count % 2 or len(ks) == 1:
            outs = []
            for i in range(count):
                node = self.leaf(zs[i], ks[0])
                for j in range(1, len(ks)):
                    node = ("add", node, self.leaf(zs[i + j], ks[j]))
                outs.append(node)
            return outs
        half = count // 2
        even, odd, k0, k1 = zs[0::2], zs[1::2], ks[0::2], ks[1::2]
        both = [self.k(("add", k0[j], k1[j])) if j < len(k1) else k0[j] for j in range(len(k0))]
        need = half + len(k0) - 1
        first = self.fast(odd[:need], both, half)
        second = self.fast([self.z(("sub", even[n], odd[n])) for n in range(need)], k0, half)
        need = half + len(k1) - 1
        third = self.fast([self.z(("sub", even[n + 1], odd[n])) for n in range(need)], k1, half)
        outs = []
        for n in range(half):
            outs += [("add", first[n], second[n]), ("add", first[n], third[n])]
        return outs


def fill(load, rows, derived, width, lane_blocks):
    last = width // SUB - 1
    for block in range(width // SUB):
        for cb in range(lane_blocks):
            lons, lanes = slice(block * SUB, (block + 1) * SUB), slice(cb * LANES, (cb + 1) * LANES)
            for n, value in enumerate(rows(lambda m: load(m, lons, lanes).astype(F32))):
                derived[cb, n, (block + 1) * SUB : (block + 2) * SUB, :] = value
                if block == 0:
                    derived[cb, n, width + SUB : width + 2 * SUB, :] = value
                if block == last:
                    derived[cb, n, 0:SUB, :] = value


def fir(derived, weights, cb, z, n, start, wide):
    lanes = slice(cb * LANES, (cb + 1) * LANES)
    total = [None] * wide
    for b in range(TAPS):
        weight = jnp.broadcast_to(weights[n, b : b + 1, lanes], (SUB, LANES))
        for v in range(wide):
            term = weight * derived[cb, z, pl.ds(start + (SUB - PAD + b + v * SUB), SUB), :]
            total[v] = term if total[v] is None else total[v] + term
    return total


def own_rows(plan):
    def rows(load):
        values = {}

        def node(z):
            if z not in values:
                op = plan.z_ops[z]
                if op[0] == "row":
                    inside = PAD <= op[1] < PAD + plan.rows
                    values[z] = load(op[1] - PAD) if inside else None
                else:
                    left, right = node(op[1]), node(op[2])
                    values[z] = left if right is None else (-right if left is None else left - right)
            return values[z]

        return [node(z) for z, _ in plan.leaves]

    return rows


def tap_rows(kernel_ref, which, plan, weights):
    values = []
    for op in plan.k_ops:
        if op[0] == "tap":
            values.append(kernel_ref[op[1], :, which, :])
        else:
            values.append(values[op[1]] + values[op[2]])
    for n, (_, k) in enumerate(plan.leaves):
        weights[n, 0:TAPS, :] = values[k]


EDGE_PRODUCTS = ((3, 1, None), (0, 0, 1), (2, 2, None), (1, 2, 1), (0, 2, None))
EDGE_OUTS = ((0, 1, 2), (0, 3), (4,))


def gelu(u):
    half = 0.5 * u
    return half + half * jnp.tanh(u * (0.7978845608028654 + 0.035677408136300125 * (u * u)))


def expand(which, total, gain, wu, bu, hidden):
    center = jnp.mean(total, axis=-1, keepdims=True)
    total = total - center
    spread = jnp.mean(total * total, axis=-1, keepdims=True)
    normed = (total * lax.rsqrt(spread + 1e-6) * gain[which : which + 1, :]).astype(BF16)
    for n in range(hidden.shape[1] // TILE):
        cols = slice(n * TILE, (n + 1) * TILE)
        u = jnp.dot(normed, wu[:, cols], preferred_element_type=F32)
        hidden[:, cols] = gelu(u + bu[which : which + 1, cols]).astype(BF16)


def contract(split, base, hidden, x_ref, wd, out, begin, size, flux_refs):
    count, width, channels = out.shape
    cols = slice(begin, begin + size)
    update = lax.dot_general(
        hidden[...], wd[cols, :], (((1,), (1,)), ((), ())), preferred_element_type=F32
    )
    for n in range(count):
        state = x_ref[base + n, :, cols].astype(F32)
        out[n, :, cols] = (state + update[n * width : (n + 1) * width]).astype(BF16)
    if flux_refs:
        fo, surf = flux_refs
        flux = jnp.dot(out[...].reshape(count * width, channels), fo[...], preferred_element_type=F32).astype(BF16)
        for n in range(count):
            row = flux[n * width : (n + 1) * width]
            if split:
                surf[:, n] = row.reshape(split, width // split, flux.shape[1])
            else:
                surf[n] = row


def surface_rows(split, ref, first, count):
    return ref.at[:, pl.ds(first, count)] if split else ref.at[pl.ds(first, count)]


def own_kernel(which, *refs):
    x_ref, kernel, *refs = refs
    number = (len(refs) - 4) // 2
    sources, acc_ref, targets = refs[:number], refs[number], refs[number + 1 : 2 * number + 1]
    derived, weights, sem = refs[2 * number + 1 :]
    rows, width, channels = x_ref.shape
    lane_blocks = channels // LANES
    plan = Plan(rows, TAPS)
    copies = [
        pltpu.make_async_copy(source.at[which] if len(source.shape) > len(target.shape) else source, target, sem.at[n])
        for n, (source, target) in enumerate(zip(sources, targets))
    ]
    for copy in copies:
        copy.start()
    tap_rows(kernel, which, plan, weights)
    wide = 2 if width % (2 * SUB) == 0 else 1
    size = wide * SUB
    combine = own_rows(plan)

    def prepare(cb, start):
        lanes = slice(cb * LANES, (cb + 1) * LANES)
        values = combine(lambda m: x_ref[m, pl.ds(start, size), lanes].astype(F32))
        for n, value in enumerate(values):
            derived[cb, n, pl.ds(start + SUB, size), :] = value

    def wrap(cb):
        for n in range(len(plan.leaves)):
            derived[cb, n, 0:SUB, :] = derived[cb, n, width : width + SUB, :]
            derived[cb, n, width + SUB : width + 2 * SUB, :] = derived[cb, n, SUB : 2 * SUB, :]

    for start in range(0, width, size):
        prepare(0, start)
    for cb in range(lane_blocks):
        lanes = slice(cb * LANES, (cb + 1) * LANES)
        wrap(cb)

        @pl.loop(0, width // size)
        def _(step):
            start = pl.multiple_of(step * size, size)
            done = {}

            def value(node):
                if node not in done:
                    if node[0] == "add":
                        left, right = value(node[1]), value(node[2])
                        done[node] = [a + b for a, b in zip(left, right)]
                    else:
                        done[node] = fir(derived, weights, cb, node[1], node[1], start, wide)
                return done[node]

            for i, node in enumerate(plan.outs):
                for v, part in enumerate(value(node)):
                    acc_ref[i, pl.ds(start + v * SUB, SUB), lanes] = part
            if cb + 1 < lane_blocks:
                prepare(cb + 1, start)

    for copy in copies:
        copy.wait()


def side_kernel(cfg, *refs):
    which, has_flux, split, first, prefetch = cfg
    refs = list(refs)
    x_ref, acc_ref, wu, wd, kernel, gain, bu, halo_ref = [refs.pop(0) for _ in range(8)]
    fo = refs.pop(0) if has_flux else None
    rows, width, channels = x_ref.shape
    middle = rows - 2 * PAD
    held = [refs.pop(0) for _ in range((1 + has_flux) * (not first))]
    sources = [refs.pop(0) for _ in range(prefetch)]
    surf = None
    if first:
        out = refs.pop(0)
        surf = refs.pop(0) if has_flux else None
        targets = [refs.pop(0) for _ in range(prefetch)]
        derived, weights, conv, hidden, sem = refs
    else:
        out_all = refs.pop(0)
        surf_all = refs.pop(0) if has_flux else None
        targets = [refs.pop(0) for _ in range(prefetch)]
        derived, weights, conv, hidden, sem, out = refs if not has_flux else (*refs, None)
    lane_blocks = channels // LANES
    before = parity() if first else 1 - parity()
    count = PAD + middle if first else PAD
    base = (1 - before) * (rows - count)

    copies = [(source, target) for source, target in zip(sources, targets)]
    if not first:
        place = before * PAD
        copies.append((held[0], out_all.at[pl.ds(place, PAD + middle)]))
        if has_flux:
            out = out_all.at[pl.ds(base, PAD)]
            copies.append((held[1], surface_rows(split, surf_all, place, PAD + middle)))
            surf = surface_rows(split, surf_all, base, PAD)
    copies = [pltpu.make_async_copy(a, b, sem.at[n]) for n, (a, b) in enumerate(copies)]
    for copy in copies:
        copy.start()

    def rows_of(load):
        d = [load(before * (PAD - 1 - j) + (1 - before) * j) for j in range(PAD)]
        return d + [d[0] + d[1]]

    def taps(j):
        return kernel[before * (PAD - 1 - j) + (1 - before) * (PAD + 1 + j), :, which, :]

    fill(lambda m, lons, lanes: halo_ref[m, lons, lanes], rows_of, derived, width, lane_blocks)
    for n, (_, add, subtract) in enumerate(EDGE_PRODUCTS):
        weights[n, 0:TAPS, :] = taps(add) if subtract is None else taps(add) - taps(subtract)
    wide = 2 if width % (2 * SUB) == 0 else 1
    for cb in range(lane_blocks):
        lanes = slice(cb * LANES, (cb + 1) * LANES)

        @pl.loop(0, width // (wide * SUB))
        def _(step):
            start = pl.multiple_of(step * (wide * SUB), wide * SUB)
            done = {}
            for j, products in enumerate(EDGE_OUTS):
                row = before * j + (1 - before) * (rows - 1 - j)
                total = [acc_ref[row, pl.ds(start + v * SUB, SUB), lanes] for v in range(wide)]
                for n in products:
                    if n not in done:
                        done[n] = fir(derived, weights, cb, EDGE_PRODUCTS[n][0], n, start, wide)
                    total = [a + b for a, b in zip(total, done[n])]
                for v in range(wide):
                    conv[row - base, pl.ds(start + v * SUB, SUB), lanes] = total[v]

    if first:
        for n in range(middle):
            conv[before * PAD + n] = acc_ref[PAD + n]
    expand(which, conv[...].reshape(count * width, channels), gain, wu, bu, hidden)
    if has_flux or first:
        contract(split, base, hidden, x_ref, wd, out, 0, channels, (fo, surf) if has_flux else None)
    else:
        for begin in range(0, channels, TILE):
            size = min(TILE, channels - begin)
            contract(split, base, hidden, x_ref, wd, out, begin, size, None)
            cols = pl.ds(begin, size)
            copies.append(
                pltpu.make_async_copy(
                    out.at[:, :, cols], out_all.at[pl.ds(base, PAD), :, cols], sem.at[len(copies)]
                )
            )
            copies[-1].start()
    for copy in copies:
        copy.wait()


def mix(which, x, halo, shared, small, flux_out=None, split=0, prefetch=(), flush=None):
    w_up, w_down = shared
    kernel, gain, b_up = small
    one, two = halo
    rows, width, channels = x.shape
    has_flux = flux_out is not None
    hidden = w_up.shape[-1]
    blocks = channels // LANES
    middle = rows - 2 * PAD

    def piece(count):
        return (split, count, width // split, depth) if split else (count, width, depth)

    def cost(count):
        cells = count * width
        return pl.CostEstimate(
            flops=4 * cells * channels * hidden, bytes_accessed=14 * cells * channels, transcendentals=cells * hidden
        )

    model = [w_up, w_down]
    loaded = [pltpu.VMEM(w_up.shape[1:], BF16), pltpu.VMEM(w_down.shape[1:], BF16)]
    if has_flux:
        depth = flux_out.shape[1]
        model.append(flux_out)
        loaded.append(pltpu.VMEM(flux_out.shape, BF16))
    leaves = len(Plan(rows, TAPS).leaves)
    out_specs = [VMEM] * (1 + len(loaded))
    in_specs = [VMEM] * 2 + [ANY] * len(model)
    model = [far(v) for v in model]
    if flush is not None:
        model.append(near(flush))
        in_specs.append(VMEM)
        loaded.append(jax.ShapeDtypeStruct(flush.shape, flush.dtype))
        out_specs.append(ANY)
    acc, *loaded = pl.pallas_call(
        functools.partial(own_kernel, which),
        out_shape=[pltpu.VMEM((rows, width, channels), F32)] + loaded,
        in_specs=in_specs,
        out_specs=out_specs,
        scratch_shapes=[
            pltpu.VMEM((blocks, leaves, width + 2 * SUB, LANES), F32),
            pltpu.VMEM((leaves, SUB, channels), F32),
            pltpu.SemaphoreType.DMA((4,)),
        ],
        compiler_params=pltpu.CompilerParams(vmem_limit_bytes=16 << 20),
        cost_estimate=pl.CostEstimate(
            flops=60 * rows * width * channels, bytes_accessed=8 * rows * width * channels, transcendentals=0
        ),
    )(near(x), near(kernel), *model)
    flushed = [loaded.pop()] if flush is not None else []

    def side(first, halo_rows, held, out_shape, prefetch):
        count = PAD + middle if first else PAD
        close = [x, acc, *loaded[:2], kernel, gain, b_up, halo_rows] + loaded[2:] + held
        scratch = [
            pltpu.VMEM((blocks, PAD + 1, width + 2 * SUB, LANES), F32),
            pltpu.VMEM((len(EDGE_PRODUCTS), SUB, channels), F32),
            pltpu.VMEM((count, width, channels), F32),
            pltpu.VMEM((count * width, hidden), BF16),
            pltpu.SemaphoreType.DMA((16,)),
        ]
        if not first:
            scratch += [] if has_flux else [pltpu.VMEM((count, width, channels), BF16)]
        return pl.pallas_call(
            functools.partial(side_kernel, (which, has_flux, split, first, len(prefetch))),
            out_shape=out_shape + [pltpu.VMEM(v.shape, v.dtype) for v in prefetch],
            in_specs=[VMEM] * len(close) + [ANY] * len(prefetch),
            out_specs=[VMEM if first or has_flux else ANY] + [VMEM] * (len(out_shape) - 1 + len(prefetch)),
            scratch_shapes=scratch,
            compiler_params=pltpu.CompilerParams(vmem_limit_bytes=LIMIT),
            cost_estimate=cost(count),
        )(*[near(v) for v in close], *[far(v) for v in prefetch])

    held_shape = [pltpu.VMEM((PAD + middle, width, channels), BF16)]
    full = pltpu.VMEM if has_flux else jax.ShapeDtypeStruct
    out_shape = [full((rows, width, channels), BF16)]
    if has_flux:
        held_shape.append(pltpu.VMEM(piece(PAD + middle), BF16))
        out_shape.append(pltpu.VMEM(piece(rows), BF16))
    held = side(True, one, [], held_shape, ())
    return [*side(False, two, list(held), out_shape, prefetch), *flushed]


def stage_kernel(number, x_hbm, *refs):
    sources, (x_ref, one_ref, two_ref), targets, sem = refs[:number], refs[number : number + 3], refs[number + 3 : -1], refs[-1]
    last = x_hbm.shape[0] - PAD
    odd = parity()
    pairs = [
        (x_hbm.at[pl.ds(odd * last, PAD)], two_ref),
        (x_hbm.at[pl.ds((1 - odd) * last, PAD)], one_ref),
        (x_hbm, x_ref),
        *zip(sources, targets),
    ]
    copies = [pltpu.make_async_copy(a, b, sem.at[n]) for n, (a, b) in enumerate(pairs)]
    for copy in copies:
        copy.start()
    for copy in copies:
        copy.wait()


def stage(x, small):
    edge = pltpu.VMEM((PAD,) + x.shape[1:], x.dtype)
    return pl.pallas_call(
        functools.partial(stage_kernel, len(small)),
        out_shape=[pltpu.VMEM(x.shape, x.dtype), edge, edge] + [pltpu.VMEM(v.shape, v.dtype) for v in small],
        in_specs=[ANY] * (1 + len(small)),
        out_specs=[VMEM] * (3 + len(small)),
        scratch_shapes=[pltpu.SemaphoreType.DMA((3 + len(small),))],
        compiler_params=pltpu.CompilerParams(vmem_limit_bytes=1 << 20),
        name="stage",
    )(far(x), *[far(v) for v in small])


def pick_kernel(partner_ref, remap_ref, x_ref, out_ref):
    bands, rows = out_ref.shape[:2]
    for o in range(bands):
        band = partner_ref[o]
        picked = [x_ref[band, remap_ref[o * rows + r]] for r in range(rows)]
        for r in range(rows):
            out_ref[o, r] = picked[r]


def pick_rows(x, partner, remap):
    if x.shape[2] % SUB:
        height = x.shape[1]
        indices = jnp.repeat(partner, height) * height + remap
        return jnp.take(x.reshape((-1,) + x.shape[2:]), indices, axis=0, mode="clip").reshape(x.shape)
    smem = pl.BlockSpec(memory_space=pltpu.SMEM)
    return pl.pallas_call(
        pick_kernel,
        out_shape=pltpu.VMEM(x.shape, x.dtype),
        in_specs=[smem, smem, VMEM],
        out_specs=VMEM,
        compiler_params=pltpu.CompilerParams(vmem_limit_bytes=1 << 20),
        name="pick",
    )(*[pltpu.with_memory_space_constraint(v, pltpu.SMEM) for v in (partner, remap)], near(x))


def ocean_in_kernel(split, ocean_ref, moved_ref, mask_ref, fi_ref, out_ref, edges_ref):
    rows, width, _ = out_ref.shape
    odd = parity()
    mask = jnp.transpose(mask_ref[...].astype(F32))
    order = list(range(PAD)) + list(range(rows - PAD, rows)) + list(range(PAD, rows - PAD))
    for i in order:
        moved = moved_ref[:, i].reshape(width, fi_ref.shape[0]) if split else moved_ref[i]
        forcing = jnp.dot(moved, fi_ref[...], preferred_element_type=F32)
        value = (ocean_ref[i].astype(F32) + mask[:, i : i + 1] * forcing).astype(BF16)
        out_ref[i] = value
        if i < PAD:
            edges_ref[1 - odd, i] = value
        if i >= rows - PAD:
            edges_ref[odd, i - rows + PAD] = value


def ocean_input(ocean, moved, mask, flux_in, split):
    rows, width, channels = ocean.shape
    return pl.pallas_call(
        functools.partial(ocean_in_kernel, split),
        out_shape=[pltpu.VMEM((rows, width, channels), BF16), pltpu.VMEM((2, PAD, width, channels), BF16)],
        in_specs=[VMEM] * 4,
        out_specs=[VMEM] * 2,
        compiler_params=pltpu.CompilerParams(vmem_limit_bytes=8 << 20),
        cost_estimate=pl.CostEstimate(
            flops=2 * rows * width * channels * flux_in.shape[0], bytes_accessed=8 * rows * width * channels, transcendentals=0
        ),
        name="ocean_in",
    )(near(ocean), near(moved), near(mask), near(flux_in))


def halos(one, two):
    size = lax.axis_size("band")
    inner = [(i, i ^ 1) for i in range(size)]
    outer = [(i, i + 1) for i in range(1, size - 1, 2)] + [(i + 1, i) for i in range(1, size - 1, 2)]
    two = lax.ppermute(two, "band", outer)
    one = lax.ppermute(one, "band", inner)
    return one, two


def per_device(
    atm_state,
    ocean_state,
    dw_kernel,
    norm_gain,
    w_up,
    b_up,
    w_down,
    flux_out,
    flux_in,
    partner,
    remap,
    land_mask,
):
    height, width, _ = atm_state.shape
    size = lax.axis_size("band")
    share = width // size
    split = size if share % SUB == 0 else 0
    shared = (w_up, w_down)

    atm, one, two, *small = stage(atm_state, [dw_kernel.transpose(1, 2, 0, 3), norm_gain, b_up])
    halo = halos(one, two)
    atm_next, surface, ocean, mask, fi = mix(
        0, atm, halo, shared, small, flux_out, split, (ocean_state, land_mask, flux_in)
    )
    if not split:
        surface = surface.reshape(height, size, share, -1).transpose(1, 0, 2, 3)
    spread = lax.all_to_all(surface, "band", split_axis=0, concat_axis=0, tiled=True)
    picked = pick_rows(spread, partner, remap)
    moved = lax.all_to_all(picked, "band", split_axis=0, concat_axis=0, tiled=True)
    if not split:
        moved = moved.transpose(1, 0, 2, 3).reshape(height, width, -1)
    ocean_in, edges = ocean_input(ocean, moved, mask, fi, split)
    halo = halos(edges[0], edges[1])
    ocean_next, atm_next = mix(1, ocean_in, halo, shared, small, flush=atm_next)
    return (atm_next, ocean_next)


def solution(mesh):
    in_specs = (
        P(("ens", "band"), None, None),
        P(("ens", "band"), None, None),
        P(),
        P(),
        P(),
        P(),
        P(),
        P(),
        P(),
        P("ens"),
        P("ens"),
        P(("ens", "band"), None),
    )
    out_specs = (P(("ens", "band"), None, None), P(("ens", "band"), None, None))

    return jax.shard_map(per_device, mesh=mesh, in_specs=in_specs, out_specs=out_specs, check_vma=False)
```

```python
import functools

import jax
import jax.numpy as jnp
from jax import lax
from jax.experimental import pallas as pl
from jax.experimental.pallas import tpu as pltpu
from jax.sharding import PartitionSpec as P


LANES = 128
SUB = 8
TAPS = 7
PAD = TAPS // 2
TILE = 256
F32 = jnp.float32
BF16 = jnp.bfloat16
VMEM = pl.BlockSpec(memory_space=pltpu.VMEM)
ANY = pl.BlockSpec(memory_space=pl.ANY)
LIMIT = 24 << 20


def parity():
    return lax.axis_index("band") % 2


def far(x):
    return pltpu.with_memory_space_constraint(x, pltpu.HBM)


def near(x):
    return pltpu.with_memory_space_constraint(x, pltpu.VMEM)


class Plan:
    def __init__(self, rows, taps):
        self.rows = rows
        self.z_ops, self.k_ops, self.leaves = [], [], []
        self.z_index, self.k_index = {}, {}
        zs = [self.z(("row", m)) for m in range(rows + taps - 1)]
        ks = [self.k(("tap", a)) for a in range(taps)]
        self.outs = self.fast(zs, ks, rows)

    def z(self, op):
        if op not in self.z_index:
            self.z_index[op] = len(self.z_ops)
            self.z_ops.append(op)
        return self.z_index[op]

    def k(self, op):
        if op not in self.k_index:
            self.k_index[op] = len(self.k_ops)
            self.k_ops.append(op)
        return self.k_index[op]

    def leaf(self, z, k):
        self.leaves.append((z, k))
        return ("leaf", len(self.leaves) - 1)

    def fast(self, zs, ks, count):
        if count % 2 or len(ks) == 1:
            outs = []
            for i in range(count):
                node = self.leaf(zs[i], ks[0])
                for j in range(1, len(ks)):
                    node = ("add", node, self.leaf(zs[i + j], ks[j]))
                outs.append(node)
            return outs
        half = count // 2
        even, odd, k0, k1 = zs[0::2], zs[1::2], ks[0::2], ks[1::2]
        both = [self.k(("add", k0[j], k1[j])) if j < len(k1) else k0[j] for j in range(len(k0))]
        need = half + len(k0) - 1
        first = self.fast(odd[:need], both, half)
        second = self.fast([self.z(("sub", even[n], odd[n])) for n in range(need)], k0, half)
        need = half + len(k1) - 1
        third = self.fast([self.z(("sub", even[n + 1], odd[n])) for n in range(need)], k1, half)
        outs = []
        for n in range(half):
            outs += [("add", first[n], second[n]), ("add", first[n], third[n])]
        return outs


def fill(load, rows, derived, width, lane_blocks):
    last = width // SUB - 1
    for block in range(width // SUB):
        for cb in range(lane_blocks):
            lons, lanes = slice(block * SUB, (block + 1) * SUB), slice(cb * LANES, (cb + 1) * LANES)
            for n, value in enumerate(rows(lambda m: load(m, lons, lanes).astype(F32))):
                derived[cb, n, (block + 1) * SUB : (block + 2) * SUB, :] = value
                if block == 0:
                    derived[cb, n, width + SUB : width + 2 * SUB, :] = value
                if block == last:
                    derived[cb, n, 0:SUB, :] = value


def fir(derived, weights, cb, z, n, start, wide):
    lanes = slice(cb * LANES, (cb + 1) * LANES)
    total = [None] * wide
    for b in range(TAPS):
        weight = jnp.broadcast_to(weights[n, b : b + 1, lanes], (SUB, LANES))
        for v in range(wide):
            term = weight * derived[cb, z, pl.ds(start + (SUB - PAD + b + v * SUB), SUB), :]
            total[v] = term if total[v] is None else total[v] + term
    return total


def own_rows(plan):
    def rows(load):
        values = {}

        def node(z):
            if z not in values:
                op = plan.z_ops[z]
                if op[0] == "row":
                    inside = PAD <= op[1] < PAD + plan.rows
                    values[z] = load(op[1] - PAD) if inside else None
                else:
                    left, right = node(op[1]), node(op[2])
                    values[z] = left if right is None else (-right if left is None else left - right)
            return values[z]

        return [node(z) for z, _ in plan.leaves]

    return rows


def tap_rows(kernel_ref, which, plan, weights):
    values = []
    for op in plan.k_ops:
        if op[0] == "tap":
            values.append(kernel_ref[op[1], :, which, :])
        else:
            values.append(values[op[1]] + values[op[2]])
    for n, (_, k) in enumerate(plan.leaves):
        weights[n, 0:TAPS, :] = values[k]


EDGE_PRODUCTS = ((3, 1, None), (0, 0, 1), (2, 2, None), (1, 2, 1), (0, 2, None))
EDGE_OUTS = ((0, 1, 2), (0, 3), (4,))


def gelu(u):
    half = 0.5 * u
    return half + half * jnp.tanh(u * (0.7978845608028654 + 0.035677408136300125 * (u * u)))


def expand(which, total, gain, wu, bu, hidden, beside=()):
    beside = list(beside)
    tiles = hidden.shape[1] // TILE
    each = -(-len(beside) // tiles)
    center = jnp.mean(total, axis=-1, keepdims=True)
    total = total - center
    spread = jnp.mean(total * total, axis=-1, keepdims=True)
    normed = (total * lax.rsqrt(spread + 1e-6) * gain[which : which + 1, :]).astype(BF16)
    for n in range(tiles):
        cols = slice(n * TILE, (n + 1) * TILE)
        u = jnp.dot(normed, wu[:, cols], preferred_element_type=F32)
        hidden[:, cols] = gelu(u + bu[which : which + 1, cols]).astype(BF16)
        for step in beside[n * each : (n + 1) * each]:
            step()


def contract(split, base, hidden, x_ref, wd, out, flux_refs, beside=(), ready=None):
    count, width, channels = out.shape
    beside = list(beside)
    parts = -(-channels // TILE)
    each = -(-len(beside) // parts)
    for part in range(parts):
        begin = part * TILE
        size = min(TILE, channels - begin)
        cols = slice(begin, begin + size)
        update = lax.dot_general(
            hidden[...], wd[cols, :], (((1,), (1,)), ((), ())), preferred_element_type=F32
        )
        for step in beside[part * each : (part + 1) * each]:
            step()
        for n in range(count):
            state = x_ref[base + n, :, cols].astype(F32)
            out[n, :, cols] = (state + update[n * width : (n + 1) * width]).astype(BF16)
        if ready is not None:
            ready(begin, size)
    if flux_refs:
        fo, surf = flux_refs
        flux = jnp.dot(out[...].reshape(count * width, channels), fo[...], preferred_element_type=F32).astype(BF16)
        for n in range(count):
            row = flux[n * width : (n + 1) * width]
            if split:
                surf[:, n] = row.reshape(split, width // split, flux.shape[1])
            else:
                surf[n] = row


def surface_rows(split, ref, first, count):
    return ref.at[:, pl.ds(first, count)] if split else ref.at[pl.ds(first, count)]


def own_kernel(which, *refs):
    x_ref, kernel, *refs = refs
    number = (len(refs) - 4) // 2
    sources, acc_ref, targets = refs[:number], refs[number], refs[number + 1 : 2 * number + 1]
    derived, weights, sem = refs[2 * number + 1 :]
    rows, width, channels = x_ref.shape
    lane_blocks = channels // LANES
    plan = Plan(rows, TAPS)
    copies = [
        pltpu.make_async_copy(source.at[which] if len(source.shape) > len(target.shape) else source, target, sem.at[n])
        for n, (source, target) in enumerate(zip(sources, targets))
    ]
    for copy in copies:
        copy.start()
    tap_rows(kernel, which, plan, weights)
    wide = 2 if width % (2 * SUB) == 0 else 1
    size = wide * SUB
    combine = own_rows(plan)

    def prepare(cb, start):
        lanes = slice(cb * LANES, (cb + 1) * LANES)
        values = combine(lambda m: x_ref[m, pl.ds(start, size), lanes].astype(F32))
        for n, value in enumerate(values):
            derived[cb, n, pl.ds(start + SUB, size), :] = value

    def wrap(cb):
        for n in range(len(plan.leaves)):
            derived[cb, n, 0:SUB, :] = derived[cb, n, width : width + SUB, :]
            derived[cb, n, width + SUB : width + 2 * SUB, :] = derived[cb, n, SUB : 2 * SUB, :]

    for start in range(0, width, size):
        prepare(0, start)
    for cb in range(lane_blocks):
        lanes = slice(cb * LANES, (cb + 1) * LANES)
        wrap(cb)

        @pl.loop(0, width // size)
        def _(step):
            start = pl.multiple_of(step * size, size)
            done = {}

            def value(node):
                if node not in done:
                    if node[0] == "add":
                        left, right = value(node[1]), value(node[2])
                        done[node] = [a + b for a, b in zip(left, right)]
                    else:
                        done[node] = fir(derived, weights, cb, node[1], node[1], start, wide)
                return done[node]

            for i, node in enumerate(plan.outs):
                for v, part in enumerate(value(node)):
                    acc_ref[i, pl.ds(start + v * SUB, SUB), lanes] = part
            if cb + 1 < lane_blocks:
                prepare(cb + 1, start)

    for copy in copies:
        copy.wait()


def halo_steps(which, before, acc_ref, halo_ref, kernel, derived, weights, conv):
    rows, width, channels = acc_ref.shape
    lane_blocks = channels // LANES

    def rows_of(load):
        d = [load(before * (PAD - 1 - j) + (1 - before) * j) for j in range(PAD)]
        return d + [d[0] + d[1]]

    def taps(j):
        return kernel[before * (PAD - 1 - j) + (1 - before) * (PAD + 1 + j), :, which, :]

    fill(lambda m, lons, lanes: halo_ref[m, lons, lanes], rows_of, derived, width, lane_blocks)
    for n, (_, add, subtract) in enumerate(EDGE_PRODUCTS):
        weights[n, 0:TAPS, :] = taps(add) if subtract is None else taps(add) - taps(subtract)
    wide = 2 if width % (2 * SUB) == 0 else 1

    def step(cb, start):
        lanes = slice(cb * LANES, (cb + 1) * LANES)
        done = {}
        for j, products in enumerate(EDGE_OUTS):
            row = before * j + (1 - before) * (rows - 1 - j)
            total = [acc_ref[row, start + v * SUB : start + (v + 1) * SUB, lanes] for v in range(wide)]
            for n in products:
                if n not in done:
                    done[n] = fir(derived, weights, cb, EDGE_PRODUCTS[n][0], n, start, wide)
                total = [a + b for a, b in zip(total, done[n])]
            for v in range(wide):
                place = before * j + (1 - before) * (PAD - 1 - j)
                conv[place, start + v * SUB : start + (v + 1) * SUB, lanes] = total[v]

    return [
        functools.partial(step, cb, start) for cb in range(lane_blocks) for start in range(0, width, wide * SUB)
    ]


def middle_kernel(which, has_flux, split, *refs):
    refs = list(refs)
    x_ref, acc_ref, wu, wd, kernel, gain, bu, halo_ref = [refs.pop(0) for _ in range(8)]
    fo = refs.pop(0) if has_flux else None
    hidden, out = refs.pop(0), refs.pop(0)
    surf = refs.pop(0) if has_flux else None
    derived, weights, near_hidden, conv = refs
    rows, width, channels = x_ref.shape
    count = rows - 2 * PAD
    steps = halo_steps(which, parity(), acc_ref, halo_ref, kernel, derived, weights, conv)
    total = acc_ref[PAD : PAD + count].reshape(count * width, channels)
    expand(which, total, gain, wu, bu, hidden, steps)
    expand(which, conv[...].reshape(PAD * width, channels), gain, wu, bu, near_hidden)
    base = (1 - parity()) * (rows - PAD)
    contract(split, base, near_hidden, x_ref, wd, out, (fo, surf) if has_flux else None)


def edges_kernel(which, has_flux, split, prefetch, *refs):
    refs = list(refs)
    x_ref, acc_ref, wu, wd, kernel, gain, bu, halo_ref = [refs.pop(0) for _ in range(8)]
    fo = refs.pop(0) if has_flux else None
    near_hidden, held = refs.pop(0), refs.pop(0)
    held_surf = refs.pop(0) if has_flux else None
    sources = [refs.pop(0) for _ in range(prefetch)]
    out_all = refs.pop(0)
    surf_all = refs.pop(0) if has_flux else None
    targets = [refs.pop(0) for _ in range(prefetch)]
    derived, weights, conv, hidden, sem = refs[:5]
    rows, width, channels = x_ref.shape
    middle = rows - 2 * PAD
    copies = []

    def start(source, target):
        copies.append(pltpu.make_async_copy(source, target, sem.at[len(copies)]))
        copies[-1].start()

    for source, target in zip(sources, targets):
        start(source, target)
    odd = parity()
    start(held, out_all.at[pl.ds((1 - odd) * (rows - PAD), PAD)])
    if has_flux:
        start(held_surf, surface_rows(split, surf_all, (1 - odd) * (rows - PAD), PAD))
    steps = halo_steps(which, 1 - odd, acc_ref, halo_ref, kernel, derived, weights, conv)
    for side, units in enumerate((near_hidden, hidden)):
        base = PAD if side == 0 else odd * (rows - PAD)
        number = middle if side == 0 else PAD
        beside = steps if side == 0 else ()
        if side == 1:
            expand(which, conv[...].reshape(PAD * width, channels), gain, wu, bu, units)
        if has_flux:
            out, surf = out_all.at[pl.ds(base, number)], surface_rows(split, surf_all, base, number)
            contract(split, base, units, x_ref, wd, out, (fo, surf), beside)
            continue
        out = refs[5].at[side, pl.ds(0, number)]

        def ready(begin, size, out=out, base=base, number=number):
            cols = pl.ds(begin, size)
            start(out.at[:, :, cols], out_all.at[pl.ds(base, number), :, cols])

        contract(split, base, units, x_ref, wd, out, None, beside, ready)
    for copy in copies:
        copy.wait()


def mix(which, x, halo, shared, small, flux_out=None, split=0, prefetch=(), flush=None):
    w_up, w_down = shared
    kernel, gain, b_up = small
    one, two = halo
    rows, width, channels = x.shape
    has_flux = flux_out is not None
    hidden = w_up.shape[-1]
    blocks = channels // LANES
    middle = rows - 2 * PAD

    def piece(count):
        return (split, count, width // split, depth) if split else (count, width, depth)

    def cost(count):
        cells = count * width
        return pl.CostEstimate(
            flops=4 * cells * channels * hidden, bytes_accessed=14 * cells * channels, transcendentals=cells * hidden
        )

    model = [w_up, w_down]
    loaded = [pltpu.VMEM(w_up.shape[1:], BF16), pltpu.VMEM(w_down.shape[1:], BF16)]
    if has_flux:
        depth = flux_out.shape[1]
        model.append(flux_out)
        loaded.append(pltpu.VMEM(flux_out.shape, BF16))
    leaves = len(Plan(rows, TAPS).leaves)
    out_specs = [VMEM] * (1 + len(loaded))
    in_specs = [VMEM] * 2 + [ANY] * len(model)
    model = [far(v) for v in model]
    if flush is not None:
        model.append(near(flush))
        in_specs.append(VMEM)
        loaded.append(jax.ShapeDtypeStruct(flush.shape, flush.dtype))
        out_specs.append(ANY)
    acc, *loaded = pl.pallas_call(
        functools.partial(own_kernel, which),
        out_shape=[pltpu.VMEM((rows, width, channels), F32)] + loaded,
        in_specs=in_specs,
        out_specs=out_specs,
        scratch_shapes=[
            pltpu.VMEM((blocks, leaves, width + 2 * SUB, LANES), F32),
            pltpu.VMEM((leaves, SUB, channels), F32),
            pltpu.SemaphoreType.DMA((4,)),
        ],
        compiler_params=pltpu.CompilerParams(vmem_limit_bytes=16 << 20),
        cost_estimate=pl.CostEstimate(
            flops=60 * rows * width * channels, bytes_accessed=8 * rows * width * channels, transcendentals=0
        ),
    )(near(x), near(kernel), *model)
    flushed = [loaded.pop()] if flush is not None else []

    full = pltpu.VMEM if has_flux else jax.ShapeDtypeStruct
    held_shape = [pltpu.VMEM((middle * width, hidden), BF16), pltpu.VMEM((PAD, width, channels), BF16)]
    out_shape = [full((rows, width, channels), BF16)]
    if has_flux:
        held_shape.append(pltpu.VMEM(piece(PAD), BF16))
        out_shape.append(pltpu.VMEM(piece(rows), BF16))
    halo_scratch = [
        pltpu.VMEM((blocks, PAD + 1, width + 2 * SUB, LANES), F32),
        pltpu.VMEM((len(EDGE_PRODUCTS), SUB, channels), F32),
    ]
    base = [x, acc, *loaded[:2], kernel, gain, b_up]
    close = base + [one] + loaded[2:]
    held = pl.pallas_call(
        functools.partial(middle_kernel, which, has_flux, split),
        out_shape=held_shape,
        in_specs=[VMEM] * len(close),
        out_specs=[VMEM] * len(held_shape),
        scratch_shapes=halo_scratch
        + [pltpu.VMEM((PAD * width, hidden), BF16), pltpu.VMEM((PAD, width, channels), F32)],
        compiler_params=pltpu.CompilerParams(vmem_limit_bytes=LIMIT),
        cost_estimate=cost(middle),
    )(*[near(v) for v in close])
    close = base + [two] + loaded[2:] + list(held)
    out = pl.pallas_call(
        functools.partial(edges_kernel, which, has_flux, split, len(prefetch)),
        out_shape=out_shape + [pltpu.VMEM(v.shape, v.dtype) for v in prefetch],
        in_specs=[VMEM] * len(close) + [ANY] * len(prefetch),
        out_specs=[VMEM if has_flux else ANY] + [VMEM] * (len(out_shape) - 1 + len(prefetch)),
        scratch_shapes=halo_scratch
        + [
            pltpu.VMEM((PAD, width, channels), F32),
            pltpu.VMEM((PAD * width, hidden), BF16),
            pltpu.SemaphoreType.DMA((16,)),
        ]
        + ([] if has_flux else [pltpu.VMEM((2, PAD, width, channels), BF16)]),
        compiler_params=pltpu.CompilerParams(vmem_limit_bytes=LIMIT),
        cost_estimate=cost(2 * PAD),
    )(*[near(v) for v in close], *[far(v) for v in prefetch])
    return [*out, *flushed]


def stage_kernel(number, x_hbm, *refs):
    sources, (x_ref, one_ref, two_ref), targets, sem = refs[:number], refs[number : number + 3], refs[number + 3 : -1], refs[-1]
    last = x_hbm.shape[0] - PAD
    odd = parity()
    pairs = [
        (x_hbm.at[pl.ds(odd * last, PAD)], two_ref),
        (x_hbm.at[pl.ds((1 - odd) * last, PAD)], one_ref),
        (x_hbm, x_ref),
        *zip(sources, targets),
    ]
    copies = [pltpu.make_async_copy(a, b, sem.at[n]) for n, (a, b) in enumerate(pairs)]
    for copy in copies:
        copy.start()
    for copy in copies:
        copy.wait()


def stage(x, small):
    edge = pltpu.VMEM((PAD,) + x.shape[1:], x.dtype)
    return pl.pallas_call(
        functools.partial(stage_kernel, len(small)),
        out_shape=[pltpu.VMEM(x.shape, x.dtype), edge, edge] + [pltpu.VMEM(v.shape, v.dtype) for v in small],
        in_specs=[ANY] * (1 + len(small)),
        out_specs=[VMEM] * (3 + len(small)),
        scratch_shapes=[pltpu.SemaphoreType.DMA((3 + len(small),))],
        compiler_params=pltpu.CompilerParams(vmem_limit_bytes=1 << 20),
        name="stage",
    )(far(x), *[far(v) for v in small])


def pick_kernel(partner_ref, remap_ref, x_ref, out_ref):
    bands, rows = out_ref.shape[:2]
    for o in range(bands):
        band = partner_ref[o]
        picked = [x_ref[band, remap_ref[o * rows + r]] for r in range(rows)]
        for r in range(rows):
            out_ref[o, r] = picked[r]


def pick_rows(x, partner, remap):
    if x.shape[2] % SUB:
        height = x.shape[1]
        indices = jnp.repeat(partner, height) * height + remap
        return jnp.take(x.reshape((-1,) + x.shape[2:]), indices, axis=0, mode="clip").reshape(x.shape)
    smem = pl.BlockSpec(memory_space=pltpu.SMEM)
    return pl.pallas_call(
        pick_kernel,
        out_shape=pltpu.VMEM(x.shape, x.dtype),
        in_specs=[smem, smem, VMEM],
        out_specs=VMEM,
        compiler_params=pltpu.CompilerParams(vmem_limit_bytes=1 << 20),
        name="pick",
    )(*[pltpu.with_memory_space_constraint(v, pltpu.SMEM) for v in (partner, remap)], near(x))


def ocean_in_kernel(split, ocean_ref, moved_ref, mask_ref, fi_ref, out_ref, edges_ref):
    rows, width, _ = out_ref.shape
    odd = parity()
    mask = jnp.transpose(mask_ref[...].astype(F32))
    order = list(range(PAD)) + list(range(rows - PAD, rows)) + list(range(PAD, rows - PAD))
    for i in order:
        moved = moved_ref[:, i].reshape(width, fi_ref.shape[0]) if split else moved_ref[i]
        forcing = jnp.dot(moved, fi_ref[...], preferred_element_type=F32)
        value = (ocean_ref[i].astype(F32) + mask[:, i : i + 1] * forcing).astype(BF16)
        out_ref[i] = value
        if i < PAD:
            edges_ref[1 - odd, i] = value
        if i >= rows - PAD:
            edges_ref[odd, i - rows + PAD] = value


def ocean_input(ocean, moved, mask, flux_in, split):
    rows, width, channels = ocean.shape
    return pl.pallas_call(
        functools.partial(ocean_in_kernel, split),
        out_shape=[pltpu.VMEM((rows, width, channels), BF16), pltpu.VMEM((2, PAD, width, channels), BF16)],
        in_specs=[VMEM] * 4,
        out_specs=[VMEM] * 2,
        compiler_params=pltpu.CompilerParams(vmem_limit_bytes=8 << 20),
        cost_estimate=pl.CostEstimate(
            flops=2 * rows * width * channels * flux_in.shape[0], bytes_accessed=8 * rows * width * channels, transcendentals=0
        ),
        name="ocean_in",
    )(near(ocean), near(moved), near(mask), near(flux_in))


def halos(one, two):
    size = lax.axis_size("band")
    inner = [(i, i ^ 1) for i in range(size)]
    outer = [(i, i + 1) for i in range(1, size - 1, 2)] + [(i + 1, i) for i in range(1, size - 1, 2)]
    two = lax.ppermute(two, "band", outer)
    one = lax.ppermute(one, "band", inner)
    return one, two


def per_device(
    atm_state,
    ocean_state,
    dw_kernel,
    norm_gain,
    w_up,
    b_up,
    w_down,
    flux_out,
    flux_in,
    partner,
    remap,
    land_mask,
):
    height, width, _ = atm_state.shape
    size = lax.axis_size("band")
    share = width // size
    split = size if share % SUB == 0 else 0
    shared = (w_up, w_down)

    atm, one, two, *small = stage(atm_state, [dw_kernel.transpose(1, 2, 0, 3), norm_gain, b_up])
    halo = halos(one, two)
    atm_next, surface, ocean, mask, fi = mix(
        0, atm, halo, shared, small, flux_out, split, (ocean_state, land_mask, flux_in)
    )
    if not split:
        surface = surface.reshape(height, size, share, -1).transpose(1, 0, 2, 3)
    spread = lax.all_to_all(surface, "band", split_axis=0, concat_axis=0, tiled=True)
    picked = pick_rows(spread, partner, remap)
    moved = lax.all_to_all(picked, "band", split_axis=0, concat_axis=0, tiled=True)
    if not split:
        moved = moved.transpose(1, 0, 2, 3).reshape(height, width, -1)
    ocean_in, edges = ocean_input(ocean, moved, mask, fi, split)
    halo = halos(edges[0], edges[1])
    ocean_next, atm_next = mix(1, ocean_in, halo, shared, small, flush=atm_next)
    return (atm_next, ocean_next)


def solution(mesh):
    in_specs = (
        P(("ens", "band"), None, None),
        P(("ens", "band"), None, None),
        P(),
        P(),
        P(),
        P(),
        P(),
        P(),
        P(),
        P("ens"),
        P("ens"),
        P(("ens", "band"), None),
    )
    out_specs = (P(("ens", "band"), None, None), P(("ens", "band"), None, None))

    return jax.shard_map(per_device, mesh=mesh, in_specs=in_specs, out_specs=out_specs, check_vma=False)
```
